128 devices in a mesh: ctx: 8 (over y, core), grp: 16 (over x, z).
Axes of the slice: x: 4, y: 4, z: 4, core: 2. Of those that a mesh axis runs over, the one named last changes fastest.
Arguments:
- query_feat: bfloat16 [32768, 4096], P(('ctx', 'grp')), may hold values from 0.0099487305 to 1
- key_feat: bfloat16 [32768, 4096], P(('ctx', 'grp')), may hold values from 0.0099487305 to 1
- values: bfloat16 [32768, 2048], P(('ctx', 'grp')), may hold values from -6 to 6
- teacher: bfloat16 [32768, 2048], P('ctx', 'grp'), may hold values from -4 to 4
Outputs:
- query_grad: bfloat16 [32768, 4096], P(('ctx', 'grp'))
- key_grad: bfloat16 [32768, 4096], P(('ctx', 'grp'))
The draws below stay inside these ranges and needn't reach their ends.
All inputs are finite; a program needn't handle non-finite values.
Results may differ from the reference program's by a relative error of at most 0.001.
Values may be sent and summed in bfloat16 or wider, within the bound.
No kernel may reach another device: no remote copies, remote signals or barrier semaphores. Data moves between devices by JAX's collectives and lax.ppermute only.
A program may use at most 576 MiB of HBM per device.

```python
import math
import jax
import jax.numpy as jnp
from jax import lax

H = 16
DH = 128
FEAT = 256
TOKENS = 32768


def block_scale(own_key, extent, shards, least, top_value):
    def one(dim, shards_of):
        draws = jax.random.uniform(jax.random.fold_in(jax.random.fold_in(own_key, 6), dim), (shards_of,), jnp.float32, least / len(shards), top_value / len(shards))
        return jnp.repeat(jnp.exp(draws), extent[dim] // shards_of).reshape((-1,) + (1,) * (len(extent) - dim - 1))

    gain = one(*shards[0])
    for cut in shards[1:]:
        gain = gain * one(*cut)
    return gain


def scatter_about(key, dims, scale, reach, cuts=(), kind=jnp.bfloat16):
    array = jax.random.normal(key, dims, jnp.float32) * scale
    if len(cuts) > 0:
        array = block_scale(key, dims, cuts, -0.22, 0.18) * array
    return jnp.clip(array, min=-reach, max=reach).astype(kind)


def setup_inputs(seed: int = 0) -> dict:
    splits = jax.random.split(jax.random.key(seed), 5)
    query_feat = jnp.clip(jnp.exp(math.log(1.0) - 4.61031033 * jax.random.uniform(splits[0], (TOKENS, H * FEAT), jnp.float32) ** block_scale(splits[0], (TOKENS, H * FEAT), ((0, 128),), -0.2, 0.2)), 0.0099487305, 1.0).astype(jnp.bfloat16)
    key_feat = jnp.clip(jnp.exp(math.log(1.0) - 4.61031033 * jax.random.uniform(splits[1], (TOKENS, H * FEAT), jnp.float32) ** block_scale(splits[1], (TOKENS, H * FEAT), ((0, 128),), -0.2, 0.2)), 0.0099487305, 1.0).astype(jnp.bfloat16)
    values = scatter_about(splits[2], (TOKENS, H * DH), 1.0, 6.0, ((0, 128),))
    teacher = scatter_about(splits[3], (TOKENS, H * DH), 0.5, 4.0, ((0, 8), (1, 16)))
    return dict(query_feat=query_feat, key_feat=key_feat, values=values, teacher=teacher)


HIGH = lax.Precision.HIGHEST


def one_head(query_one, key_one, value_one, teacher_one, block):
    count = query_one.shape[0] // block
    feat = query_one.shape[1]
    width = value_one.shape[1]
    qs = query_one.reshape(count, block, feat)
    ks = key_one.reshape(count, block, feat)
    vs = value_one.reshape(count, block, width)
    ys = teacher_one.reshape(count, block, width)
    rows_t = lax.broadcasted_iota(jnp.int32, (block, block), 0)
    rows_s = lax.broadcasted_iota(jnp.int32, (block, block), 1)
    causal = (rows_s <= rows_t).astype(jnp.float32)

    def forward(carry, piece):
        kv_now, key_now = carry
        q, k, v, y = piece
        scores = jnp.dot(q, k.T, precision=HIGH) * causal
        numer = jnp.dot(scores, v, precision=HIGH) + jnp.dot(q, kv_now, precision=HIGH)
        denom = jnp.sum(scores, axis=1) + jnp.dot(q, key_now, precision=HIGH)
        student = numer / denom[:, None]
        resid = student - y
        d_numer = resid / denom[:, None]
        d_denom = -jnp.sum(resid * student, axis=1) / denom
        mixed = (jnp.dot(d_numer, v.T, precision=HIGH) + d_denom[:, None]) * causal
        q_grad = jnp.dot(mixed, k, precision=HIGH) + jnp.dot(d_numer, kv_now.T, precision=HIGH) + d_denom[:, None] * key_now[None, :]
        new_carry = (kv_now + jnp.dot(k.T, v, precision=HIGH), key_now + jnp.sum(k, axis=0))
        return new_carry, (q_grad, d_numer, d_denom)

    start = (jnp.zeros((feat, width), jnp.float32), jnp.zeros((feat,), jnp.float32))
    unused, (q_grads, d_numers, d_denoms) = lax.scan(forward, start, (qs, ks, vs, ys))

    def backward(carry, piece):
        after_kv, after_q = carry
        q, k, v, d_numer, d_denom = piece
        mixed = (jnp.dot(d_numer, v.T, precision=HIGH) + d_denom[:, None]) * causal
        k_grad = jnp.dot(mixed.T, q, precision=HIGH) + jnp.dot(v, after_kv.T, precision=HIGH) + after_q[None, :]
        new_carry = (after_kv + jnp.dot(q.T, d_numer, precision=HIGH), after_q + jnp.dot(d_denom, q, precision=HIGH))
        return new_carry, k_grad

    unused_two, k_grads = lax.scan(backward, start, (qs, ks, vs, d_numers, d_denoms), reverse=True)
    return q_grads.reshape(-1, feat), k_grads.reshape(-1, feat)


def reference(query_feat, key_feat, values, teacher):
    block = math.gcd(TOKENS, 512)
    scale = float(TOKENS) ** 0.5
    query3 = query_feat.reshape(TOKENS, H, FEAT)
    key3 = key_feat.reshape(TOKENS, H, FEAT)
    value3 = values.reshape(TOKENS, H, DH)
    teacher3 = teacher.reshape(TOKENS, H, DH)

    def per_head(head):
        query_one = lax.dynamic_index_in_dim(query3, head, 1, False).astype(jnp.float32)
        key_one = lax.dynamic_index_in_dim(key3, head, 1, False).astype(jnp.float32)
        value_one = lax.dynamic_index_in_dim(value3, head, 1, False).astype(jnp.float32)
        teacher_one = lax.dynamic_index_in_dim(teacher3, head, 1, False).astype(jnp.float32)
        q_grad, k_grad = one_head(query_one, key_one, value_one, teacher_one, block)
        return (scale * q_grad).astype(jnp.bfloat16), (scale * k_grad).astype(jnp.bfloat16)

    q_all, k_all = lax.map(per_head, jnp.arange(H, dtype=jnp.int32))
    query_grad = jnp.transpose(q_all, (1, 0, 2)).reshape(TOKENS, H * FEAT)
    key_grad = jnp.transpose(k_all, (1, 0, 2)).reshape(TOKENS, H * FEAT)
    return query_grad, key_grad
```

```python
import functools

import jax
import jax.numpy as jnp
from jax import lax
from jax.experimental import pallas as pl
from jax.experimental.pallas import tpu as pltpu
from jax.sharding import PartitionSpec as P

NX, NZ, NY = 4, 4, 4
HL = 4
TB = 256
F = 256
D = 128
SR = D + 8
BF, F32 = jnp.bfloat16, jnp.float32
VMEM_LIMIT = 60 * 1024 * 1024
ANY = pl.ANY


def grp_pairs(dx, dz):
    return [(x * NZ + z, ((x + dx) % NX) * NZ + (z + dz) % NZ) for x in range(NX) for z in range(NZ)]


def y_pairs(d):
    return [(y * 2 + c, (y + d) * 2 + c) for y in range(NY) for c in range(2) if 0 <= y + d < NY]


CORE_PAIRS = [(y * 2 + c, y * 2 + 1 - c) for y in range(NY) for c in range(2)]


def params():
    return pltpu.CompilerParams(vmem_limit_bytes=VMEM_LIMIT)


def nn(a, b):
    return lax.dot_general(a, b, (((1,), (0,)), ((), ())), preferred_element_type=F32)


def nt(a, b):
    return lax.dot_general(a, b, (((1,), (1,)), ((), ())), preferred_element_type=F32)


def tn(a, b):
    return lax.dot_general(a, b, (((0,), (0,)), ((), ())), preferred_element_type=F32)


def split(x):
    hi = x.astype(BF)
    return hi, (x - hi.astype(F32)).astype(BF)


def mod4(a):
    return lax.rem(a + 8, 4)


def pack_kv_kernel(pos, k_ref, v_ref, *outs):
    z = pos[1]
    for r in range(NZ):
        zd = mod4(z + r)
        outs[r][0, :, 0:F] = k_ref[:, pl.ds(pl.multiple_of(zd * F, F), F)]
        outs[r][0, :, F : F + D] = v_ref[:, pl.ds(pl.multiple_of(zd * D, D), D)]


def pack_kv(pos, k, v):
    return pl.pallas_call(
        pack_kv_kernel,
        out_shape=[jax.ShapeDtypeStruct((HL, TB, F + D), BF)] * NZ,
        grid_spec=pltpu.PrefetchScalarGridSpec(
            num_scalar_prefetch=1,
            grid=(HL,),
            in_specs=[
                pl.BlockSpec((TB, NZ * F), lambda j, p: (0, j)),
                pl.BlockSpec((TB, NZ * D), lambda j, p: (0, j)),
            ],
            out_specs=[pl.BlockSpec((1, TB, F + D), lambda j, p: (j, 0, 0))] * NZ,
        ),
        compiler_params=params(),
        name="pack_kv",
    )(pos, k, v)


def pack_q_kernel(pos, q_ref, *outs):
    z = pos[1]
    for r in range(NZ):
        zd = mod4(z + r)
        outs[r][0] = q_ref[:, pl.ds(pl.multiple_of(zd * F, F), F)]


def pack_q(pos, q):
    return pl.pallas_call(
        pack_q_kernel,
        out_shape=[jax.ShapeDtypeStruct((HL, TB, F), BF)] * NZ,
        grid_spec=pltpu.PrefetchScalarGridSpec(
            num_scalar_prefetch=1,
            grid=(HL,),
            in_specs=[pl.BlockSpec((TB, NZ * F), lambda j, p: (0, j))],
            out_specs=[pl.BlockSpec((1, TB, F), lambda j, p: (j, 0, 0))] * NZ,
        ),
        compiler_params=params(),
        name="pack_q",
    )(pos, q)


def unpack_kernel(pos, *refs):
    z = pos[1]
    out = refs[NZ]
    for r in range(NZ):
        zs = mod4(z - r)
        out[:, pl.ds(pl.multiple_of(zs * F, F), F)] = refs[r][0]


def unpack(pos, parts):
    return pl.pallas_call(
        unpack_kernel,
        out_shape=jax.ShapeDtypeStruct((TB, HL * NZ * F), BF),
        grid_spec=pltpu.PrefetchScalarGridSpec(
            num_scalar_prefetch=1,
            grid=(HL,),
            in_specs=[pl.BlockSpec((1, TB, F), lambda j, p: (j, 0, 0))] * NZ,
            out_specs=pl.BlockSpec((TB, NZ * F), lambda j, p: (0, j)),
        ),
        compiler_params=params(),
        name="unpack",
    )(pos, *parts)


def sums_kernel(pos, *refs):
    x = pos[0]
    kvs, outs = refs[:NZ], refs[NZ:]
    ones = jnp.ones((8, TB), BF)
    for r in range(NX):
        hd = mod4(x + r)
        kv = jnp.zeros((D, F), F32)
        ks = jnp.zeros((8, F), F32)
        for b in range(NZ):
            k = kvs[b][hd, :, 0:F]
            v = kvs[b][hd, :, F : F + D]
            kv = kv + tn(v, k)
            ks = ks + nn(ones, k)
        outs[r][0:D, :] = kv
        outs[r][D:SR, :] = ks


def line_sums(pos, kvs):
    return pl.pallas_call(
        sums_kernel,
        out_shape=[jax.ShapeDtypeStruct((SR, F), F32)] * NX,
        grid_spec=pltpu.PrefetchScalarGridSpec(
            num_scalar_prefetch=1,
            grid=(1,),
            in_specs=[pl.BlockSpec((HL, TB, F + D), lambda i, p: (0, 0, 0))] * NZ,
            out_specs=[pl.BlockSpec((SR, F), lambda i, p: (0, 0))] * NX,
        ),
        compiler_params=params(),
        name="line_sums",
    )(pos, *kvs)


def full_state(ref):
    return jnp.concatenate([ref[0:D, :], jnp.broadcast_to(ref[D : D + 1, :], (D, F))], axis=0)


def augmented(v):
    return jnp.concatenate([v, jnp.ones((TB, D), BF)], axis=1)


def causal_mask():
    t = lax.broadcasted_iota(jnp.int32, (TB, TB), 0)
    s = lax.broadcasted_iota(jnp.int32, (TB, TB), 1)
    return s <= t


def forward_kernel(scale, pos, *refs):
    kvs, qs, teas, states = refs[0:4], refs[4:8], refs[8:12], refs[12:16]
    qouts, sums, dhi_out, dlo_out = refs[16:20], refs[20:24], refs[24], refs[25]
    kv_s, q_s, t_s, g_s, in_sem, out_sem = refs[26:32]
    x, z = pos[0], pos[1]

    def incoming(r):
        hd = mod4(x - r)
        copies = []
        for b in range(NZ):
            zs = mod4(z - b)
            copies.append(pltpu.make_async_copy(kvs[b].at[hd], kv_s.at[r, zs], in_sem.at[r, b, 0]))
            copies.append(pltpu.make_async_copy(qs[b].at[hd], q_s.at[r, zs], in_sem.at[r, b, 1]))
        copies.append(pltpu.make_async_copy(teas[r], t_s.at[r], in_sem.at[r, 0, 2]))
        return copies

    for r in range(HL):
        for c in incoming(r):
            c.start()

    mask = causal_mask()
    sent = []
    for r in range(HL):
        hd = mod4(x - r)
        for c in incoming(r):
            c.wait()
        st = full_state(states[r])
        adj = jnp.zeros((2 * D, F), F32)
        for j in range(NZ):
            q = q_s[r, j]
            k = kv_s[r, j, :, 0:F]
            va = augmented(kv_s[r, j, :, F : F + D])
            sc = jnp.where(mask, nt(q, k), 0.0)
            s_hi, s_lo = split(sc)
            st_hi, st_lo = split(st)
            nd = nn(s_hi, va) + nn(s_lo, va) + nt(q, st_hi) + nt(q, st_lo)
            numer, denom = nd[:, 0:D], nd[:, D:]
            student = numer / denom
            resid = student - t_s[r, j * TB : (j + 1) * TB, :].astype(F32)
            dn = resid / denom
            dd = -jnp.sum(resid * student, axis=1, keepdims=True) / denom
            d_hi, d_lo = split(jnp.concatenate([dn, dd * (1.0 / D)], axis=1))
            dhi_out[hd, j] = d_hi
            dlo_out[hd, j] = d_lo
            mixed = jnp.where(mask, nt(d_hi, va) + nt(d_lo, va), 0.0)
            m_hi, m_lo = split(mixed)
            qg = nn(m_hi, k) + nn(m_lo, k) + nn(d_hi, st_hi) + nn(d_lo, st_hi) + nn(d_hi, st_lo)
            g_s[r, j] = (qg * scale).astype(BF)
            adj = adj + tn(d_hi, q) + tn(d_lo, q)
            if j < NZ - 1:
                st = st + tn(va, k)
        for b in range(NZ):
            c = pltpu.make_async_copy(g_s.at[r, mod4(z + b)], qouts[b].at[hd], out_sem.at[r, b])
            c.start()
            sent.append(c)
        sums[(-r) % NX][...] = adj[0:SR, :]
    for c in sent:
        c.wait()


def forward(pos, kvs, qs, teas, states, scale):
    any_spec = pl.BlockSpec(memory_space=ANY)
    whole = lambda *s: pl.BlockSpec(s, lambda i, p: (0,) * len(s))
    out = pl.pallas_call(
        functools.partial(forward_kernel, scale),
        out_shape=[jax.ShapeDtypeStruct((HL, TB, F), BF)] * NZ
        + [jax.ShapeDtypeStruct((SR, F), F32)] * NX
        + [jax.ShapeDtypeStruct((HL, NZ, TB, 2 * D), BF)] * 2,
        grid_spec=pltpu.PrefetchScalarGridSpec(
            num_scalar_prefetch=1,
            grid=(1,),
            in_specs=[any_spec] * 12 + [whole(SR, F)] * 4,
            out_specs=[any_spec] * 4 + [whole(SR, F)] * 4 + [whole(HL, NZ, TB, 2 * D)] * 2,
            scratch_shapes=[
                pltpu.VMEM((HL, NZ, TB, F + D), BF),
                pltpu.VMEM((HL, NZ, TB, F), BF),
                pltpu.VMEM((HL, NZ * TB, D), BF),
                pltpu.VMEM((HL, NZ, TB, F), BF),
                pltpu.SemaphoreType.DMA((HL, NZ, 3)),
                pltpu.SemaphoreType.DMA((HL, NZ)),
            ],
        ),
        compiler_params=params(),
        name="forward",
    )(pos, *kvs, *qs, *teas, *states)
    return out[0:4], out[4:8], out[8], out[9]


def inner_kernel(pos, *refs):
    kvs, qs, dhi, dlo, out = refs[0:4], refs[4:8], refs[8], refs[9], refs[10]
    kv_s, q_s, in_sem = refs[11:14]
    z = pos[1]

    def incoming(h):
        copies = []
        for b in range(NZ):
            zs = mod4(z - b)
            copies.append(pltpu.make_async_copy(kvs[b].at[h], kv_s.at[h, zs], in_sem.at[h, b, 0]))
            copies.append(pltpu.make_async_copy(qs[b].at[h], q_s.at[h, zs], in_sem.at[h, b, 1]))
        return copies

    for h in range(HL):
        for c in incoming(h):
            c.start()
    mask = causal_mask()
    for h in range(HL):
        for c in incoming(h):
            c.wait()
        adj = None
        for j in reversed(range(NZ)):
            q = q_s[h, j]
            va = augmented(kv_s[h, j, :, F : F + D])
            d_hi, d_lo = dhi[h, j], dlo[h, j]
            m_hi, m_lo = split(jnp.where(mask, nt(d_hi, va) + nt(d_lo, va), 0.0))
            kg = tn(m_hi, q) + tn(m_lo, q)
            if adj is not None:
                a_hi, a_lo = split(adj)
                kg = kg + nn(va, a_hi) + nn(va, a_lo)
            out[h, j] = kg
            if j > 0:
                new = tn(d_hi, q) + tn(d_lo, q)
                adj = new if adj is None else adj + new


def inner(pos, kvs, qs, dhi, dlo):
    any_spec = pl.BlockSpec(memory_space=ANY)
    whole = lambda *s: pl.BlockSpec(s, lambda i, p: (0,) * len(s))
    return pl.pallas_call(
        inner_kernel,
        out_shape=jax.ShapeDtypeStruct((HL, NZ, TB, F), F32),
        grid_spec=pltpu.PrefetchScalarGridSpec(
            num_scalar_prefetch=1,
            grid=(1,),
            in_specs=[any_spec] * 8 + [whole(HL, NZ, TB, 2 * D)] * 2,
            out_specs=whole(HL, NZ, TB, F),
            scratch_shapes=[
                pltpu.VMEM((HL, NZ, TB, F + D), BF),
                pltpu.VMEM((HL, NZ, TB, F), BF),
                pltpu.SemaphoreType.DMA((HL, NZ, 2)),
            ],
        ),
        compiler_params=params(),
        name="inner",
    )(pos, *kvs, *qs, dhi, dlo)


def last_kernel(scale, pos, *refs):
    kvs, part, states, outs = refs[0:4], refs[4], refs[5:9], refs[9:13]
    x, z = pos[0], pos[1]
    for r in range(HL):
        hd = mod4(x - r)
        a_hi, a_lo = split(full_state(states[r]))
        for b in range(NZ):
            va = augmented(kvs[b][hd, :, F : F + D])
            kg = part[hd, mod4(z - b)] + nn(va, a_hi) + nn(va, a_lo)
            outs[(-b) % NZ][hd] = (kg * scale).astype(BF)


def last(pos, kvs, part, states, scale):
    whole = lambda *s: pl.BlockSpec(s, lambda i, p: (0,) * len(s))
    return pl.pallas_call(
        functools.partial(last_kernel, scale),
        out_shape=[jax.ShapeDtypeStruct((HL, TB, F), BF)] * NZ,
        grid_spec=pltpu.PrefetchScalarGridSpec(
            num_scalar_prefetch=1,
            grid=(1,),
            in_specs=[whole(HL, TB, F + D)] * 4 + [whole(HL, NZ, TB, F)] + [whole(SR, F)] * 4,
            out_specs=[whole(HL, TB, F)] * NZ,
        ),
        compiler_params=params(),
        name="last",
    )(pos, *kvs, part, *states)


def exchange_z(parts):
    far = lax.ppermute(parts[2], "grp", grp_pairs(0, 2))
    up = lax.ppermute(parts[1], "grp", grp_pairs(0, 1))
    down = lax.ppermute(parts[3], "grp", grp_pairs(0, 3))
    return [parts[0], up, far, down]


def exchange_x(parts):
    far = lax.ppermute(parts[2], "grp", grp_pairs(2, 0))
    up = lax.ppermute(parts[1], "grp", grp_pairs(1, 0))
    down = lax.ppermute(parts[3], "grp", grp_pairs(3, 0))
    return [parts[0], up, far, down]


def scan_states(sums, x, c, reverse):
    mine = exchange_x(sums)
    total = mine[0] + mine[1] + mine[2] + mine[3]
    sign = -1 if reverse else 1
    others = [lax.ppermute(total, "ctx", y_pairs(sign * d)) for d in (1, 2, 3)]
    outer = others[0] + others[1] + others[2]
    first = c == (1 if reverse else 0)
    other_core = lax.ppermute(outer + jnp.where(first, total, 0.0), "ctx", CORE_PAIRS)
    outer = outer + other_core
    back = []
    for r in range(NX):
        to = mod4(x + r)
        acc = outer
        for s in range(NX):
            at = mod4(x - s)
            take = (at > to) if reverse else (at < to)
            acc = acc + jnp.where(take, mine[s], 0.0)
        back.append(acc)
    return exchange_x(back)


def on_device(query_feat, key_feat, values, teacher):
    total_tokens = query_feat.shape[0] * lax.axis_size("ctx") * lax.axis_size("grp")
    scale = float(total_tokens) ** 0.5
    g = lax.axis_index("grp").astype(jnp.int32)
    x, z = g // NZ, lax.rem(g, NZ)
    c = lax.rem(lax.axis_index("ctx").astype(jnp.int32), 2)
    pos = jnp.stack([x, z])
    kvs = exchange_z(pack_kv(pos, key_feat, values))
    qs = exchange_z(pack_q(pos, query_feat))
    line = NZ * TB
    teas = exchange_x([lax.dynamic_slice(teacher, (mod4(x + r) * line, 0), (line, D)) for r in range(NX)])
    states = scan_states(line_sums(pos, kvs), x, c, False)
    q_parts, adj_sums, d_hi, d_lo = forward(pos, kvs, qs, teas, states, scale)
    query_grad = unpack(pos, exchange_z(q_parts))
    part = inner(pos, kvs, qs, d_hi, d_lo)
    after = scan_states(adj_sums, x, c, True)
    key_grad = unpack(pos, exchange_z(last(pos, kvs, part, after, scale)))
    return query_grad, key_grad


def solution(mesh):
    placed = (
        P(("ctx", "grp"), None),
        P(("ctx", "grp"), None),
        P(("ctx", "grp"), None),
        P("ctx", "grp"),
    )
    return jax.shard_map(
        on_device,
        mesh=mesh,
        in_specs=placed,
        out_specs=(P(("ctx", "grp"), None), P(("ctx", "grp"), None)),
        check_vma=False,
    )
```

```python
import functools

import jax
import jax.numpy as jnp
from jax import lax
from jax.experimental import pallas as pl
from jax.experimental.pallas import tpu as pltpu
from jax.sharding import PartitionSpec as P


NX, NZ, NY = 4, 4, 4
HL = 4
TB = 256
F = 256
D = 128
SR = D + 8
BF, F32 = jnp.bfloat16, jnp.float32
VMEM_LIMIT = 8 * 1024 * 1024


def grp_pairs(dx, dz):
    return [(x * NZ + z, ((x + dx) % NX) * NZ + (z + dz) % NZ) for x in range(NX) for z in range(NZ)]


def y_pairs(d):
    return [(y * 2 + c, ((y + d) % NY) * 2 + c) for y in range(NY) for c in range(2)]


CORE_PAIRS = [(y * 2 + c, y * 2 + 1 - c) for y in range(NY) for c in range(2)]


def params():
    return pltpu.CompilerParams(vmem_limit_bytes=VMEM_LIMIT)


def nn(a, b):
    return lax.dot_general(a, b, (((1,), (0,)), ((), ())), preferred_element_type=F32)


def nt(a, b):
    return lax.dot_general(a, b, (((1,), (1,)), ((), ())), preferred_element_type=F32)


def tn(a, b):
    return lax.dot_general(a, b, (((0,), (0,)), ((), ())), preferred_element_type=F32)


def split(x):
    hi = x.astype(BF)
    return hi, (x - hi.astype(F32)).astype(BF)


def mod4(a):
    return lax.rem(a + 8, 4)


def vmem(n):
    return [pl.BlockSpec(memory_space=pltpu.VMEM)] * n


def hbm(n):
    return [pl.BlockSpec(memory_space=pltpu.HBM)] * n


def place():
    return [pl.BlockSpec(memory_space=pltpu.SMEM)]


def shape(*dims, kind=F32):
    return jax.ShapeDtypeStruct(dims, kind)


def piece(cols):
    return shape(HL, TB, cols, kind=BF)


def call(kernel, out_shape, in_specs, out_specs, args, scratch=()):
    return pl.pallas_call(
        kernel,
        out_shape=out_shape,
        in_specs=in_specs,
        out_specs=out_specs,
        scratch_shapes=list(scratch),
        compiler_params=params(),
    )(*args)


def run_copies(copies):
    for c in copies:
        c.start()
    for c in copies:
        c.wait()


def pack_kv_kernel(shifts, pos, k_ref, v_ref, *refs):
    outs, sem = refs[:-1], refs[-1]
    z = pos[1]
    copies = []
    for i, r in enumerate(shifts):
        zd = mod4(z + r)
        for j in range(HL):
            kc = pl.ds(pl.multiple_of((j * NZ + zd) * F, F), F)
            vc = pl.ds(pl.multiple_of((j * NZ + zd) * D, D), D)
            copies.append(pltpu.make_async_copy(k_ref.at[:, kc], outs[i].at[j, :, 0:F], sem.at[i, j, 0]))
            copies.append(pltpu.make_async_copy(v_ref.at[:, vc], outs[i].at[j, :, F : F + D], sem.at[i, j, 1]))
    run_copies(copies)


def pack_kv(pos, k, v, shifts):
    n = len(shifts)
    return call(
        functools.partial(pack_kv_kernel, shifts),
        [piece(F + D)] * n,
        place() + hbm(2),
        vmem(n),
        (pos, k, v),
        [pltpu.SemaphoreType.DMA((n, HL, 2))],
    )


def pack_q_kernel(shifts, pos, q_ref, *refs):
    outs, sem = refs[:-1], refs[-1]
    z = pos[1]
    copies = []
    for i, r in enumerate(shifts):
        for j in range(HL):
            qc = pl.ds(pl.multiple_of((j * NZ + mod4(z + r)) * F, F), F)
            copies.append(pltpu.make_async_copy(q_ref.at[:, qc], outs[i].at[j], sem.at[i, j]))
    run_copies(copies)


def pack_q(pos, q, shifts):
    n = len(shifts)
    return call(
        functools.partial(pack_q_kernel, shifts),
        [piece(F)] * n,
        place() + hbm(1),
        vmem(n),
        (pos, q),
        [pltpu.SemaphoreType.DMA((n, HL))],
    )


def pack_teacher_kernel(pos, t_ref, *refs):
    outs, sem = refs[:-1], refs[-1]
    n = NZ * TB
    copies = []
    for r in range(NX):
        rows = pl.ds(pl.multiple_of(mod4(pos[0] + r) * n, n), n)
        copies.append(pltpu.make_async_copy(t_ref.at[rows, :], outs[r], sem.at[r]))
    run_copies(copies)


def pack_teacher(pos, teacher):
    return call(
        pack_teacher_kernel,
        [shape(NZ * TB, D, kind=BF)] * NX,
        place() + hbm(1),
        vmem(NX),
        (pos, teacher),
        [pltpu.SemaphoreType.DMA((NX,))],
    )


def unpack_kernel(pos, *refs):
    parts, out = refs[0:NZ], refs[NZ]
    z = pos[1]
    for r in (0, 2, 1, 3):
        for j in range(HL):
            out[:, pl.ds(pl.multiple_of((j * NZ + mod4(z - r)) * F, F), F)] = parts[r][j]


def unpack_all(pos, parts):
    return call(
        unpack_kernel,
        shape(TB, HL * NZ * F, kind=BF),
        place() + vmem(NZ),
        pl.BlockSpec(),
        (pos, *parts),
    )


def block_state(k, v):
    return jnp.concatenate([tn(v, k), nn(jnp.ones((8, TB), BF), k)], axis=0)


def sums_a_kernel(pos, kv0, kv2, out):
    for r in range(NX):
        hd = mod4(pos[0] + r)
        acc = jnp.zeros((SR, F), F32)
        for kv in (kv0, kv2):
            acc = acc + block_state(kv[hd, :, 0:F], kv[hd, :, F : F + D])
        out[r] = acc


def sums_a(pos, kv0, kv2):
    return call(sums_a_kernel, shape(NX, SR, F), place() + vmem(2), vmem(1)[0], (pos, kv0, kv2))


def sums_b_kernel(pos, kv1, kv3, part, *outs):
    for r in range(NX):
        hd = mod4(pos[0] + r)
        acc = part[r]
        for kv in (kv1, kv3):
            acc = acc + block_state(kv[hd, :, 0:F], kv[hd, :, F : F + D])
        outs[r][...] = acc


def sums_b(pos, kv1, kv3, part):
    return call(
        sums_b_kernel, [shape(SR, F)] * NX, place() + vmem(3), vmem(NX), (pos, kv1, kv3, part)
    )


def full_state(ref):
    return jnp.concatenate([ref[0:D, :], jnp.broadcast_to(ref[D : D + 1, :], (D, F))], axis=0)


def augmented(v):
    return jnp.concatenate([v, jnp.ones((TB, D), BF)], axis=1)


def causal_mask():
    t = lax.broadcasted_iota(jnp.int32, (TB, TB), 0)
    s = lax.broadcasted_iota(jnp.int32, (TB, TB), 1)
    return s <= t


def order_sums(z, parts, reverse):
    out = []
    for b in range(NZ):
        acc = jnp.zeros(parts[0].shape, F32)
        for o in range(NZ):
            if o == b:
                continue
            mine, other = mod4(z - b), mod4(z - o)
            take = (other > mine) if reverse else (other < mine)
            acc = acc + parts[o] * take.astype(F32)
        out.append(acc)
    return out


def rows_of(x):
    return jnp.concatenate(split(x), axis=0)


def halves(x):
    n = x.shape[0] // 2
    return x[:n] + x[n:]


def lines_kernel(pos, *refs):
    kvs, l_out = refs[0:4], refs[4]
    x, z = pos[0], pos[1]
    for r in range(HL):
        hd = mod4(x - r)
        parts = [block_state(kvs[b][hd, :, 0:F], kvs[b][hd, :, F : F + D]) for b in range(NZ)]
        for b, line in enumerate(order_sums(z, parts, False)):
            l_out[r, b] = line


def earlier_in_line(pos, kvs):
    return call(lines_kernel, shape(HL, NZ, SR, F), place() + vmem(4), vmem(1)[0], (pos, *kvs))


def pre_kernel(pos, *refs):
    kvs, qs, lines, nd_out = refs[0:4], refs[4:8], refs[8], refs[9]
    x = pos[0]
    mask = causal_mask()
    for r in range(HL):
        hd = mod4(x - r)
        for b in range(NZ):
            q, k = qs[b][hd], kvs[b][hd, :, 0:F]
            va = augmented(kvs[b][hd, :, F : F + D])
            st_hi, st_lo = split(full_state(lines[r, b]))
            sc = rows_of(jnp.where(mask, nt(q, k), 0.0))
            nd_out[r, b] = halves(nn(sc, va)) + nt(q, st_hi) + nt(q, st_lo)


def pre(pos, kvs, qs, lines):
    return call(
        pre_kernel, shape(HL, NZ, TB, 2 * D), place() + vmem(9), vmem(1)[0], (pos, *kvs, *qs, lines)
    )


def post_kernel(pos, *refs):
    qs, nd, teas, states = refs[0:4], refs[4], refs[5:9], refs[9:13]
    dhi_out, dlo_out, adj_out, sums = refs[13], refs[14], refs[15], refs[16:20]
    x, z = pos[0], pos[1]
    for r in range(HL):
        hd = mod4(x - r)
        e_hi, e_lo = split(full_state(states[r]))
        total = jnp.zeros((SR, F), F32)
        for b in range(NZ):
            q = qs[b][hd]
            both = nd[r, b] + nt(q, e_hi) + nt(q, e_lo)
            inverse = 1.0 / both[:, D:]
            student = both[:, 0:D] * inverse
            rows = pl.ds(pl.multiple_of(mod4(z - b) * TB, TB), TB)
            resid = student - teas[r][rows, :].astype(F32)
            dn = resid * inverse
            dd = -jnp.sum(resid * student, axis=1, keepdims=True) * inverse
            d_hi, d_lo = split(jnp.concatenate([dn, dd * (1.0 / D)], axis=1))
            dhi_out[r, b] = d_hi
            dlo_out[r, b] = d_lo
            adj = tn(d_hi, q)[0:SR] + tn(d_lo, q)[0:SR]
            adj_out[r, b] = adj
            total = total + adj
        sums[(-r) % NX][...] = total


def post(pos, qs, nd, teas, states):
    out = call(
        post_kernel,
        [shape(HL, NZ, TB, 2 * D, kind=BF)] * 2 + [shape(HL, NZ, SR, F)] + [shape(SR, F)] * NX,
        place() + vmem(13),
        vmem(3 + NX),
        (pos, *qs, nd, *teas, *states),
    )
    return out[0], out[1], out[2], out[3:7]


def qgrad_kernel(scale, pos, *refs):
    kvs, dhi, dlo, lines, states, outs = refs[0:4], refs[4], refs[5], refs[6], refs[7:11], refs[11:15]
    x = pos[0]
    mask = causal_mask()
    for r in range(HL):
        hd = mod4(x - r)
        for b in range(NZ):
            k = kvs[b][hd, :, 0:F]
            va = augmented(kvs[b][hd, :, F : F + D])
            d_hi = dhi[r, b]
            d_rows = jnp.concatenate([d_hi, dlo[r, b]], axis=0)
            mixed = rows_of(jnp.where(mask, halves(nt(d_rows, va)), 0.0))
            st_hi, st_lo = split(full_state(states[r][...] + lines[r, b]))
            qg = halves(nn(mixed, k) + nn(d_rows, st_hi)) + nn(d_hi, st_lo)
            outs[(-b) % NZ][hd] = (qg * scale).astype(BF)


def qgrad(pos, kvs, dhi, dlo, lines, states, scale):
    return call(
        functools.partial(qgrad_kernel, scale),
        [piece(F)] * NZ,
        place() + vmem(11),
        vmem(NZ),
        (pos, *kvs, dhi, dlo, lines, *states),
    )


def inner_kernel(pos, *refs):
    kvs, qs, dhi, dlo, adj, out = refs[0:4], refs[4:8], refs[8], refs[9], refs[10], refs[11]
    x, z = pos[0], pos[1]
    mask = causal_mask()
    for r in range(HL):
        hd = mod4(x - r)
        lines = order_sums(z, [adj[r, b] for b in range(NZ)], True)
        for b in range(NZ):
            q = qs[b][hd]
            va = augmented(kvs[b][hd, :, F : F + D])
            d_rows = jnp.concatenate([dhi[r, b], dlo[r, b]], axis=0)
            m_hi, m_lo = split(jnp.where(mask, halves(nt(d_rows, va)), 0.0))
            a_hi, a_lo = split(full_state(lines[b]))
            out[r, b] = tn(m_hi, q) + tn(m_lo, q) + nn(va, a_hi) + nn(va, a_lo)


def inner(pos, kvs, qs, dhi, dlo, adj):
    return call(
        inner_kernel,
        shape(HL, NZ, TB, F),
        place() + vmem(11),
        vmem(1)[0],
        (pos, *kvs, *qs, dhi, dlo, adj),
    )


def last_kernel(scale, blocks, pos, *refs):
    n = len(blocks)
    kvs, part, states, outs = refs[0:n], refs[n], refs[n + 1 : n + 5], refs[n + 5 :]
    x = pos[0]
    for r in range(HL):
        hd = mod4(x - r)
        a_hi, a_lo = split(full_state(states[r]))
        for i, b in enumerate(blocks):
            va = augmented(kvs[i][hd, :, F : F + D])
            kg = part[r, b] + nn(va, a_hi) + nn(va, a_lo)
            outs[i][hd] = (kg * scale).astype(BF)


def last(pos, kvs, part, states, scale, blocks):
    n = len(blocks)
    return call(
        functools.partial(last_kernel, scale, blocks),
        [piece(F)] * n,
        place() + vmem(n + 5),
        vmem(n),
        (pos, *[kvs[b] for b in blocks], part, *states),
    )


def send_z(part, r):
    return lax.ppermute(part, "grp", grp_pairs(0, r))


def send_x(part, r):
    return lax.ppermute(part, "grp", grp_pairs(r, 0))


def exchange_z(parts):
    far, up, down = send_z(parts[2], 2), send_z(parts[1], 1), send_z(parts[3], 3)
    return [parts[0], up, far, down]


def exchange_x(parts):
    far, up, down = send_x(parts[2], 2), send_x(parts[1], 1), send_x(parts[3], 3)
    return [parts[0], up, far, down]


def total_kernel(m0, m1, m2, m3, out):
    out[...] = (m0[...] + m1[...]) + (m2[...] + m3[...])


def core_kernel(reverse, pos, o1, o2, o3, total, outer, other):
    y, c = pos[2], pos[3]
    acc = jnp.zeros((SR, F), F32)
    for d, o in ((1, o1), (2, o2), (3, o3)):
        at = mod4(y - d)
        take = (at > y) if reverse else (at < y)
        acc = acc + o[...] * take.astype(F32)
    outer[...] = acc
    first = (c == (1 if reverse else 0)).astype(F32)
    other[...] = acc + total[...] * first


def back_kernel(reverse, pos, outer, other_core, *refs):
    mine, outs = refs[0:NX], refs[NX:]
    x = pos[0]
    base = outer[...] + other_core[...]
    for r in range(NX):
        to = mod4(x + r)
        acc = base
        for s in range(NX):
            at = mod4(x - s)
            take = (at > to) if reverse else (at < to)
            acc = acc + mine[s][...] * take.astype(F32)
        outs[r][...] = acc


def scan_states(sums, pos, reverse):
    one = shape(SR, F)
    mine = exchange_x(sums)
    total = call(total_kernel, one, vmem(4), vmem(1)[0], mine)
    others = [lax.ppermute(total, "ctx", y_pairs(d)) for d in (1, 2, 3)]
    outer, mixed = call(
        functools.partial(core_kernel, reverse), [one] * 2, place() + vmem(4), vmem(2), (pos, *others, total)
    )
    other_core = lax.ppermute(mixed, "ctx", CORE_PAIRS)
    back = call(
        functools.partial(back_kernel, reverse),
        [one] * NX,
        place() + vmem(2 + NX),
        vmem(NX),
        (pos, outer, other_core, *mine),
    )
    return exchange_x(back)


def local_step(query_feat, key_feat, values, teacher):
    total_tokens = query_feat.shape[0] * lax.axis_size("ctx") * lax.axis_size("grp")
    scale = float(total_tokens) ** 0.5
    g = lax.axis_index("grp").astype(jnp.int32)
    x, z = g // NZ, lax.rem(g, NZ)
    t = lax.axis_index("ctx").astype(jnp.int32)
    pos = jnp.stack([x, z, t // 2, lax.rem(t, 2)])
    query_feat, key_feat, values, teacher = (
        pltpu.with_memory_space_constraint(a, pltpu.HBM) for a in (query_feat, key_feat, values, teacher)
    )
    kv = [None] * NZ
    kv[2], kv[1], kv[3] = pack_kv(pos, key_feat, values, (2, 1, 3))
    (kv[0],) = pack_kv(pos, key_feat, values, (0,))
    kvs = exchange_z(kv)
    q = [None] * NZ
    q[2], q[1], q[3] = pack_q(pos, query_feat, (2, 1, 3))
    (q[0],) = pack_q(pos, query_feat, (0,))
    qs = exchange_z(q)
    teas = exchange_x(pack_teacher(pos, teacher))
    sums = sums_b(pos, kvs[1], kvs[3], sums_a(pos, kvs[0], kvs[2]))
    lines = earlier_in_line(pos, kvs)
    nd = pre(pos, kvs, qs, lines)
    states = scan_states(sums, pos, False)
    d_hi, d_lo, adj, adj_sums = post(pos, qs, nd, teas, states)
    qparts = qgrad(pos, kvs, d_hi, d_lo, lines, states, scale)
    query_grad = unpack_all(pos, exchange_z(qparts))
    part = inner(pos, kvs, qs, d_hi, d_lo, adj)
    after = scan_states(adj_sums, pos, True)
    kg = [None] * NZ
    (kg[2],) = last(pos, kvs, part, after, scale, (2,))
    kg[3], kg[1] = last(pos, kvs, part, after, scale, (1, 3))
    (kg[0],) = last(pos, kvs, part, after, scale, (0,))
    key_grad = unpack_all(pos, exchange_z(kg))
    return query_grad, key_grad


def solution(mesh):
    placed = (
        P(("ctx", "grp"), None),
        P(("ctx", "grp"), None),
        P(("ctx", "grp"), None),
        P("ctx", "grp"),
    )
    return jax.shard_map(
        local_step,
        mesh=mesh,
        in_specs=placed,
        out_specs=(P(("ctx", "grp"), None), P(("ctx", "grp"), None)),
        check_vma=False,
    )
```

```python
import functools

import jax
import jax.numpy as jnp
from jax import lax
from jax.experimental import pallas as pl
from jax.experimental.pallas import tpu as pltpu
from jax.sharding import PartitionSpec as P


NX, NZ, NY = 4, 4, 4
HL = 4
YR = 72
TB = 256
F = 256
D = 128
SR = D + 8
BF, F32 = jnp.bfloat16, jnp.float32
VMEM_LIMIT = 8 * 1024 * 1024


def grp_pairs(dx, dz):
    return [(x * NZ + z, ((x + dx) % NX) * NZ + (z + dz) % NZ) for x in range(NX) for z in range(NZ)]


def y_pairs(d):
    return [(y * 2 + c, ((y + (d if c == 0 else -d)) % NY) * 2 + c) for y in range(NY) for c in range(2)]


CORE_PAIRS = [(y * 2 + c, y * 2 + 1 - c) for y in range(NY) for c in range(2)]


def params():
    return pltpu.CompilerParams(vmem_limit_bytes=VMEM_LIMIT)


def nn(a, b):
    return lax.dot_general(a, b, (((1,), (0,)), ((), ())), preferred_element_type=F32)


def nt(a, b):
    return lax.dot_general(a, b, (((1,), (1,)), ((), ())), preferred_element_type=F32)


def tn(a, b):
    return lax.dot_general(a, b, (((0,), (0,)), ((), ())), preferred_element_type=F32)


def split(x):
    hi = x.astype(BF)
    return hi, (x - hi.astype(F32)).astype(BF)


def mod4(a):
    return lax.rem(a + 8, 4)


def vmem(n):
    return [pl.BlockSpec(memory_space=pltpu.VMEM)] * n


def hbm(n):
    return [pl.BlockSpec(memory_space=pltpu.HBM)] * n


HERE = object()


def here():
    g, t = lax.axis_index("grp").astype(jnp.int32), lax.axis_index("ctx").astype(jnp.int32)
    return lax.div(g, NZ), lax.rem(g, NZ), lax.div(t, 2), lax.rem(t, 2)


def shape(*dims, kind=F32):
    return jax.ShapeDtypeStruct(dims, kind)


def piece(cols):
    return shape(HL, TB, cols, kind=BF)


def call(kernel, out_shape, in_specs, out_specs, args, scratch=()):
    body = kernel
    if args[0] is HERE:
        args = args[1:]

        def body(*refs):
            kernel(here(), *refs)

    return pl.pallas_call(
        body,
        out_shape=out_shape,
        in_specs=in_specs,
        out_specs=out_specs,
        scratch_shapes=list(scratch),
        compiler_params=params(),
    )(*args)


def run_copies(copies):
    for c in copies:
        c.start()
    for c in copies:
        c.wait()


def pack_kv_kernel(shifts, k_ref, v_ref, *refs):
    outs, sem = refs[:-1], refs[-1]
    z = lax.rem(lax.axis_index("grp").astype(jnp.int32), NZ)
    copies = []
    for i, r in enumerate(shifts):
        zd = mod4(z + r)
        for j in range(HL):
            kc = pl.ds(pl.multiple_of((j * NZ + zd) * F, F), F)
            vc = pl.ds(pl.multiple_of((j * NZ + zd) * D, D), D)
            copies.append(pltpu.make_async_copy(k_ref.at[:, kc], outs[i].at[j, :, 0:F], sem.at[i, j, 0]))
            copies.append(pltpu.make_async_copy(v_ref.at[:, vc], outs[i].at[j, :, F : F + D], sem.at[i, j, 1]))
    run_copies(copies)


def pack_kv(k, v, shifts):
    n = len(shifts)
    return call(
        functools.partial(pack_kv_kernel, shifts),
        [piece(F + D)] * n,
        hbm(2),
        vmem(n),
        (k, v),
        [pltpu.SemaphoreType.DMA((n, HL, 2))],
    )


def pack_q_kernel(shifts, pos, q_ref, *refs):
    outs, sem = refs[:-1], refs[-1]
    z = pos[1]
    copies = []
    for i, r in enumerate(shifts):
        for j in range(HL):
            qc = pl.ds(pl.multiple_of((j * NZ + mod4(z + r)) * F, F), F)
            copies.append(pltpu.make_async_copy(q_ref.at[:, qc], outs[i].at[j], sem.at[i, j]))
    run_copies(copies)


def pack_q(pos, q, shifts):
    n = len(shifts)
    return call(
        functools.partial(pack_q_kernel, shifts),
        [piece(F)] * n,
        hbm(1),
        vmem(n),
        (pos, q),
        [pltpu.SemaphoreType.DMA((n, HL))],
    )


def pack_teacher_kernel(pos, t_ref, *refs):
    outs, sem = refs[:-1], refs[-1]
    n = NZ * TB
    copies = []
    for r in range(NX):
        rows = pl.ds(pl.multiple_of(mod4(pos[0] + r) * n, n), n)
        copies.append(pltpu.make_async_copy(t_ref.at[rows, :], outs[r], sem.at[r]))
    run_copies(copies)


def pack_teacher(pos, teacher):
    return call(
        pack_teacher_kernel,
        [shape(NZ * TB, D, kind=BF)] * NX,
        hbm(1),
        vmem(NX),
        (pos, teacher),
        [pltpu.SemaphoreType.DMA((NX,))],
    )


UR = 64


def unpack_kernel(pos, *refs):
    parts, out, held, sem = refs[0:NZ], refs[NZ], refs[NZ + 1], refs[NZ + 2]
    z = pos[1]
    copies = []
    for i in range(TB // UR):
        rows = slice(i * UR, (i + 1) * UR)
        for r in range(NZ):
            for j in range(HL):
                held[rows, pl.ds(pl.multiple_of((j * NZ + mod4(z - r)) * F, F), F)] = parts[r][j, rows, :]
        copies.append(pltpu.make_async_copy(held.at[rows, :], out.at[rows, :], sem.at[i]))
        copies[-1].start()
    for c in copies:
        c.wait()


def unpack_all(pos, parts):
    return call(
        unpack_kernel,
        shape(TB, HL * NZ * F, kind=BF),
        vmem(NZ),
        hbm(1)[0],
        (pos, *parts),
        [pltpu.VMEM((TB, HL * NZ * F), BF), pltpu.SemaphoreType.DMA((TB // UR,))],
    )


def block_state(k, v):
    return jnp.concatenate([tn(v, k), nn(jnp.ones((8, TB), BF), k)], axis=0)


def sums_a_kernel(pos, kv0, kv2, out):
    for r in range(NX):
        hd = mod4(pos[0] + r)
        acc = jnp.zeros((SR, F), F32)
        for kv in (kv0, kv2):
            acc = acc + block_state(kv[hd, :, 0:F], kv[hd, :, F : F + D])
        out[r] = acc


def sums_a(pos, kv0, kv2):
    return call(sums_a_kernel, shape(NX, SR, F), vmem(2), vmem(1)[0], (pos, kv0, kv2))


def sums_b_kernel(pos, kv1, kv3, part, *outs):
    for r in range(NX):
        hd = mod4(pos[0] + r)
        acc = part[r]
        for kv in (kv1, kv3):
            acc = acc + block_state(kv[hd, :, 0:F], kv[hd, :, F : F + D])
        outs[r][...] = acc


def sums_b(pos, kv1, kv3, part):
    return call(sums_b_kernel, [shape(SR, F)] * NX, vmem(3), vmem(NX), (pos, kv1, kv3, part))


def full_state(ref):
    return jnp.concatenate([ref[0:D, :], jnp.broadcast_to(ref[D : D + 1, :], (D, F))], axis=0)


def augmented(v):
    return jnp.concatenate([v, jnp.ones((TB, D), BF)], axis=1)


def causal_mask():
    t = lax.broadcasted_iota(jnp.int32, (TB, TB), 0)
    s = lax.broadcasted_iota(jnp.int32, (TB, TB), 1)
    return s <= t


def order_sums(z, parts, reverse):
    out = []
    for b in range(NZ):
        acc = jnp.zeros(parts[0].shape, F32)
        for o in range(NZ):
            if o == b:
                continue
            mine, other = mod4(z - b), mod4(z - o)
            take = (other > mine) if reverse else (other < mine)
            acc = acc + parts[o] * take.astype(F32)
        out.append(acc)
    return out


def rows_of(x):
    return jnp.concatenate(split(x), axis=0)


def halves(x):
    n = x.shape[0] // 2
    return x[:n] + x[n:]


def lines_kernel(pos, *refs):
    kvs, l_out = refs[0:4], refs[4]
    x, z = pos[0], pos[1]
    for r in range(HL):
        hd = mod4(x - r)
        parts = [block_state(kvs[b][hd, :, 0:F], kvs[b][hd, :, F : F + D]) for b in range(NZ)]
        for b, line in enumerate(order_sums(z, parts, False)):
            l_out[r, b] = line


def earlier_in_line(pos, kvs):
    return call(lines_kernel, shape(HL, NZ, SR, F), vmem(4), vmem(1)[0], (pos, *kvs))


def pre_kernel(pos, *refs):
    kvs, qs, lines, nd_out = refs[0:4], refs[4:8], refs[8], refs[9]
    x = pos[0]
    mask = causal_mask()
    for r in range(HL):
        hd = mod4(x - r)
        for b in range(NZ):
            q, k = qs[b][hd], kvs[b][hd, :, 0:F]
            va = augmented(kvs[b][hd, :, F : F + D])
            st_hi, st_lo = split(full_state(lines[r, b]))
            sc = rows_of(jnp.where(mask, nt(q, k), 0.0))
            nd_out[r, b] = halves(nn(sc, va)) + nt(q, st_hi) + nt(q, st_lo)


def pre(pos, kvs, qs, lines):
    return call(pre_kernel, shape(HL, NZ, TB, 2 * D), vmem(9), vmem(1)[0], (pos, *kvs, *qs, lines))


PR = 64


def post_kernel(pos, *refs):
    qs, nd, teas, states = refs[0:4], refs[4], refs[5:9], refs[9:13]
    dhi_out, dlo_out, adj_out, sums, both_s = refs[13], refs[14], refs[15], refs[16:20], refs[20]
    x, z = pos[0], pos[1]
    for r in range(HL):
        hd = mod4(x - r)
        e_hi, e_lo = split(full_state(states[r]))
        total = jnp.zeros((SR, F), F32)
        for b in range(NZ):
            q = qs[b][hd]
            held = both_s.at[b % 2]
            held[...] = nd[r, b] + nt(q, e_hi) + nt(q, e_lo)
            for i in range(TB // PR):
                rows = slice(i * PR, (i + 1) * PR)
                inverse = 1.0 / held[rows, D:]
                student = held[rows, 0:D] * inverse
                there = pl.ds(pl.multiple_of(mod4(z - b) * TB + i * PR, PR), PR)
                resid = student - teas[r][there, :].astype(F32)
                n_hi, n_lo = split(resid * inverse)
                dd = -jnp.sum(resid * student, axis=1, keepdims=True) * inverse
                c_hi, c_lo = split(dd * (1.0 / D))
                dhi_out[r, b, rows, 0:D] = n_hi
                dhi_out[r, b, rows, D:] = c_hi
                dlo_out[r, b, rows, 0:D] = n_lo
                dlo_out[r, b, rows, D:] = c_lo
            sides = tn(jnp.concatenate([dhi_out[r, b, :, 0:D], dlo_out[r, b, :, 0:D]], axis=1), q)
            ends = tn(dhi_out[r, b, :, D : D + 8], q) + tn(dlo_out[r, b, :, D : D + 8], q)
            adj = jnp.concatenate([sides[0:D] + sides[D:], ends], axis=0)
            adj_out[r, b] = adj
            total = total + adj
        sums[(-r) % NX][...] = total


def post(pos, qs, nd, teas, states):
    out = call(
        post_kernel,
        [shape(HL, NZ, TB, 2 * D, kind=BF)] * 2 + [shape(HL, NZ, SR, F)] + [shape(SR, F)] * NX,
        vmem(13),
        vmem(3 + NX),
        (pos, *qs, nd, *teas, *states),
        [pltpu.VMEM((2, TB, 2 * D), F32)],
    )
    return out[0], out[1], out[2], out[3:7]


def qgrad_kernel(scale, blocks, pos, *refs):
    n = len(blocks)
    kvs, dhi, dlo, lines, states = refs[0:n], refs[n], refs[n + 1], refs[n + 2], refs[n + 3 : n + 7]
    outs, mixed_out = refs[n + 7 : 2 * n + 7], refs[2 * n + 7]
    x = pos[0]
    mask = causal_mask()
    for r in range(HL):
        hd = mod4(x - r)
        for i, b in enumerate(blocks):
            k = kvs[i][hd, :, 0:F]
            va = augmented(kvs[i][hd, :, F : F + D])
            d_hi = dhi[r, b]
            d_rows = jnp.concatenate([d_hi, dlo[r, b]], axis=0)
            mixed = rows_of(jnp.where(mask, halves(nt(d_rows, va)), 0.0))
            mixed_out[r, i] = mixed
            st_hi, st_lo = split(full_state(states[r][...] + lines[r, b]))
            qg = halves(nn(mixed, k) + nn(d_rows, st_hi)) + nn(d_hi, st_lo)
            outs[i][hd] = (qg * scale).astype(BF)


def qgrad(pos, kvs, dhi, dlo, lines, states, scale, blocks):
    n = len(blocks)
    out = call(
        functools.partial(qgrad_kernel, scale, blocks),
        [piece(F)] * n + [shape(HL, n, 2 * TB, TB, kind=BF)],
        vmem(n + 7),
        vmem(n + 1),
        (pos, *[kvs[b] for b in blocks], dhi, dlo, lines, *states),
    )
    return out[0:n], out[n]


REST = (1, 3, 0)


def inner_kernel(pos, *refs):
    kvs, qs, far, rest, adj, out = refs[0:4], refs[4:8], refs[8], refs[9], refs[10], refs[11]
    x, z = pos[0], pos[1]
    for r in range(HL):
        hd = mod4(x - r)
        lines = order_sums(z, [adj[r, b] for b in range(NZ)], True)
        for b in range(NZ):
            q = qs[b][hd]
            va = augmented(kvs[b][hd, :, F : F + D])
            mixed = far.at[r, 0] if b == 2 else rest.at[r, REST.index(b)]
            a_hi, a_lo = split(full_state(lines[b]))
            out[r, b] = tn(mixed[0:TB, :], q) + tn(mixed[TB:, :], q) + nn(va, a_hi) + nn(va, a_lo)


def inner(pos, kvs, qs, far, rest, adj):
    return call(inner_kernel, shape(HL, NZ, TB, F), vmem(11), vmem(1)[0], (pos, *kvs, *qs, far, rest, adj))


def last_kernel(scale, blocks, pos, *refs):
    n = len(blocks)
    kvs, part, states, outs = refs[0:n], refs[n], refs[n + 1 : n + 5], refs[n + 5 :]
    x = pos[0]
    for r in range(HL):
        hd = mod4(x - r)
        a_hi, a_lo = split(full_state(states[r]))
        for i, b in enumerate(blocks):
            va = augmented(kvs[i][hd, :, F : F + D])
            kg = part[r, b] + nn(va, a_hi) + nn(va, a_lo)
            outs[i][hd] = (kg * scale).astype(BF)


def last(pos, kvs, part, states, scale, blocks):
    n = len(blocks)
    return call(
        functools.partial(last_kernel, scale, blocks),
        [piece(F)] * n,
        vmem(n + 5),
        vmem(n),
        (pos, *[kvs[b] for b in blocks], part, *states),
    )


def send_z(part, r):
    return lax.ppermute(part, "grp", grp_pairs(0, r))


def send_x(part, r):
    return lax.ppermute(part, "grp", grp_pairs(r, 0))


def exchange_z(parts):
    far, up, down = send_z(parts[2], 2), send_z(parts[1], 1), send_z(parts[3], 3)
    return [parts[0], up, far, down]


def exchange_x(parts):
    far, up, down = send_x(parts[2], 2), send_x(parts[1], 1), send_x(parts[3], 3)
    return [parts[0], up, far, down]


def total_kernel(m0, m1, m2, m3, out):
    out[...] = (m0[...] + m1[...]) + (m2[...] + m3[...])


def chip_kernel(pos, total, other, out, half):
    out[...] = total[...] + other[...]
    half[...] = out[pl.ds(pl.multiple_of(pos[3] * (SR - YR), 8), YR), :]


def spans_kernel(reverse, pos, near, far, out):
    y, c = pos[2], pos[3]

    def wanted(at):
        return ((at > y) if reverse else (at < y)).astype(F32)

    out[...] = near[...] * wanted(mod4(y - 1 + 2 * c))
    far_wanted = wanted(mod4(y + 2))
    mine = c.astype(F32)
    out[0:YR, :] += far[...] * (far_wanted * (1.0 - mine))
    out[YR:SR, :] += far[2 * YR - SR :, :] * (far_wanted * mine)


def back_kernel(reverse, pos, base_a, base_b, other, *refs):
    mine, outs = refs[0:NX], refs[NX:]
    x, c = pos[0], pos[3]
    second = (c == (0 if reverse else 1)).astype(F32)
    base = base_a[...] + base_b[...] + other[...] * second
    for r in range(NX):
        to = mod4(x + r)
        acc = base
        for s in range(NX):
            at = mod4(x - s)
            take = (at > to) if reverse else (at < to)
            acc = acc + mine[s][...] * take.astype(F32)
        outs[r][...] = acc


def scan_states(sums, pos, reverse):
    one = shape(SR, F)
    mine = exchange_x(sums)
    total = call(total_kernel, one, vmem(4), vmem(1)[0], mine)
    other = lax.ppermute(total, "ctx", CORE_PAIRS)
    chip, half = call(chip_kernel, [one, shape(YR, F)], vmem(2), vmem(2), (pos, total, other))
    far = lax.ppermute(half, "ctx", y_pairs(2))
    near = lax.ppermute(chip, "ctx", y_pairs(1))
    base = call(functools.partial(spans_kernel, reverse), one, vmem(2), vmem(1)[0], (pos, near, far))
    base_other = lax.ppermute(base, "ctx", CORE_PAIRS)
    back = call(
        functools.partial(back_kernel, reverse),
        [one] * NX,
        vmem(3 + NX),
        vmem(NX),
        (pos, base, base_other, other, *mine),
    )
    return exchange_x(back)


def local_step(query_feat, key_feat, values, teacher):
    total_tokens = query_feat.shape[0] * lax.axis_size("ctx") * lax.axis_size("grp")
    scale = float(total_tokens) ** 0.5
    pos = HERE
    query_feat, key_feat, values, teacher = (
        pltpu.with_memory_space_constraint(a, pltpu.HBM) for a in (query_feat, key_feat, values, teacher)
    )
    kv = [None] * NZ
    (kv[2],) = pack_kv(key_feat, values, (2,))
    kv[1], kv[3] = pack_kv(key_feat, values, (1, 3))
    (kv[0],) = pack_kv(key_feat, values, (0,))
    kvs = exchange_z(kv)
    q = [None] * NZ
    q[2], q[1], q[3] = pack_q(pos, query_feat, (2, 1, 3))
    (q[0],) = pack_q(pos, query_feat, (0,))
    qs = exchange_z(q)
    teas = exchange_x(pack_teacher(pos, teacher))
    sums = sums_b(pos, kvs[1], kvs[3], sums_a(pos, kvs[0], kvs[2]))
    lines = earlier_in_line(pos, kvs)
    nd = pre(pos, kvs, qs, lines)
    states = scan_states(sums, pos, False)
    d_hi, d_lo, adj, adj_sums = post(pos, qs, nd, teas, states)
    qparts = [None] * NZ
    (qparts[2],), far = qgrad(pos, kvs, d_hi, d_lo, lines, states, scale, (2,))
    (qparts[3], qparts[1], qparts[0]), rest = qgrad(pos, kvs, d_hi, d_lo, lines, states, scale, REST)
    query_grad = unpack_all(pos, exchange_z(qparts))
    part = inner(pos, kvs, qs, far, rest, adj)
    after = scan_states(adj_sums, pos, True)
    kg = [None] * NZ
    (kg[2],) = last(pos, kvs, part, after, scale, (2,))
    kg[3], kg[1] = last(pos, kvs, part, after, scale, (1, 3))
    (kg[0],) = last(pos, kvs, part, after, scale, (0,))
    key_grad = unpack_all(pos, exchange_z(kg))
    return query_grad, key_grad


def solution(mesh):
    placed = (
        P(("ctx", "grp"), None),
        P(("ctx", "grp"), None),
        P(("ctx", "grp"), None),
        P("ctx", "grp"),
    )
    return jax.shard_map(
        local_step,
        mesh=mesh,
        in_specs=placed,
        out_specs=(P(("ctx", "grp"), None), P(("ctx", "grp"), None)),
        check_vma=False,
    )
```

```python
import functools

import jax
import jax.numpy as jnp
from jax import lax
from jax.experimental import pallas as pl
from jax.experimental.pallas import tpu as pltpu
from jax.sharding import PartitionSpec as P


NX, NZ, NY = 4, 4, 4
HL = 4
YR = 72
TB = 256
F = 256
D = 128
SR = D + 8
BF, F32 = jnp.bfloat16, jnp.float32
VMEM_LIMIT = 8 * 1024 * 1024


def grp_pairs(dx, dz):
    return [(x * NZ + z, ((x + dx) % NX) * NZ + (z + dz) % NZ) for x in range(NX) for z in range(NZ)]


def y_pairs(d):
    return [(y * 2 + c, ((y + (d if c == 0 else -d)) % NY) * 2 + c) for y in range(NY) for c in range(2)]


CORE_PAIRS = [(y * 2 + c, y * 2 + 1 - c) for y in range(NY) for c in range(2)]


def params():
    return pltpu.CompilerParams(vmem_limit_bytes=VMEM_LIMIT)


def nn(a, b):
    return lax.dot_general(a, b, (((1,), (0,)), ((), ())), preferred_element_type=F32)


def nt(a, b):
    return lax.dot_general(a, b, (((1,), (1,)), ((), ())), preferred_element_type=F32)


def tn(a, b):
    return lax.dot_general(a, b, (((0,), (0,)), ((), ())), preferred_element_type=F32)


def split(x):
    hi = x.astype(BF)
    return hi, (x - hi.astype(F32)).astype(BF)


def mod4(a):
    return lax.rem(a + 8, 4)


def vmem(n):
    return [pl.BlockSpec(memory_space=pltpu.VMEM)] * n


def hbm(n):
    return [pl.BlockSpec(memory_space=pltpu.HBM)] * n


HERE = object()


def here():
    g, t = lax.axis_index("grp").astype(jnp.int32), lax.axis_index("ctx").astype(jnp.int32)
    return lax.div(g, NZ), lax.rem(g, NZ), lax.div(t, 2), lax.rem(t, 2)


def shape(*dims, kind=F32):
    return jax.ShapeDtypeStruct(dims, kind)


def piece(cols):
    return shape(HL, TB, cols, kind=BF)


def call(kernel, out_shape, in_specs, out_specs, args, scratch=()):
    body = kernel
    if args[0] is HERE:
        args = args[1:]

        def body(*refs):
            kernel(here(), *refs)

    return pl.pallas_call(
        body,
        out_shape=out_shape,
        in_specs=in_specs,
        out_specs=out_specs,
        scratch_shapes=list(scratch),
        compiler_params=params(),
    )(*args)


def run_copies(copies):
    for c in copies:
        c.start()
    for c in copies:
        c.wait()


def pack_kv_kernel(shifts, k_ref, v_ref, *refs):
    outs, sem = refs[:-1], refs[-1]
    z = lax.rem(lax.axis_index("grp").astype(jnp.int32), NZ)
    copies = []
    for i, r in enumerate(shifts):
        zd = mod4(z + r)
        for j in range(HL):
            kc = pl.ds(pl.multiple_of((j * NZ + zd) * F, F), F)
            vc = pl.ds(pl.multiple_of((j * NZ + zd) * D, D), D)
            copies.append(pltpu.make_async_copy(k_ref.at[:, kc], outs[i].at[j, :, 0:F], sem.at[i, j, 0]))
            copies.append(pltpu.make_async_copy(v_ref.at[:, vc], outs[i].at[j, :, F : F + D], sem.at[i, j, 1]))
    run_copies(copies)


def pack_kv(k, v, shifts):
    n = len(shifts)
    return call(
        functools.partial(pack_kv_kernel, shifts),
        [piece(F + D)] * n,
        hbm(2),
        vmem(n),
        (k, v),
        [pltpu.SemaphoreType.DMA((n, HL, 2))],
    )


def pack_q_kernel(shifts, pos, q_ref, *refs):
    outs, sem = refs[:-1], refs[-1]
    z = pos[1]
    copies = []
    for i, r in enumerate(shifts):
        for j in range(HL):
            qc = pl.ds(pl.multiple_of((j * NZ + mod4(z + r)) * F, F), F)
            copies.append(pltpu.make_async_copy(q_ref.at[:, qc], outs[i].at[j], sem.at[i, j]))
    run_copies(copies)


def pack_q(pos, q, shifts):
    n = len(shifts)
    return call(
        functools.partial(pack_q_kernel, shifts),
        [piece(F)] * n,
        hbm(1),
        vmem(n),
        (pos, q),
        [pltpu.SemaphoreType.DMA((n, HL))],
    )


def pack_teacher_kernel(pos, t_ref, *refs):
    outs, sem = refs[:-1], refs[-1]
    n = NZ * TB
    copies = []
    for r in range(NX):
        rows = pl.ds(pl.multiple_of(mod4(pos[0] + r) * n, n), n)
        copies.append(pltpu.make_async_copy(t_ref.at[rows, :], outs[r], sem.at[r]))
    run_copies(copies)


def pack_teacher(pos, teacher):
    return call(
        pack_teacher_kernel,
        [shape(NZ * TB, D, kind=BF)] * NX,
        hbm(1),
        vmem(NX),
        (pos, teacher),
        [pltpu.SemaphoreType.DMA((NX,))],
    )


UR = 64


def unpack_kernel(pos, *refs):
    parts, out, held, sem = refs[0:NZ], refs[NZ], refs[NZ + 1], refs[NZ + 2]
    z = pos[1]
    copies = []
    for i in range(TB // UR):
        rows = slice(i * UR, (i + 1) * UR)
        for r in range(NZ):
            for j in range(HL):
                held[rows, pl.ds(pl.multiple_of((j * NZ + mod4(z - r)) * F, F), F)] = parts[r][j, rows, :]
        copies.append(pltpu.make_async_copy(held.at[rows, :], out.at[rows, :], sem.at[i]))
        copies[-1].start()
    for c in copies:
        c.wait()


def unpack_all(pos, parts):
    return call(
        unpack_kernel,
        shape(TB, HL * NZ * F, kind=BF),
        vmem(NZ),
        hbm(1)[0],
        (pos, *parts),
        [pltpu.VMEM((TB, HL * NZ * F), BF), pltpu.SemaphoreType.DMA((TB // UR,))],
    )


def block_state(k, v):
    return jnp.concatenate([tn(v, k), nn(jnp.ones((8, TB), BF), k)], axis=0)


def sums_a_kernel(pos, kv0, kv2, out):
    for r in range(NX):
        hd = mod4(pos[0] + r)
        acc = jnp.zeros((SR, F), F32)
        for kv in (kv0, kv2):
            acc = acc + block_state(kv[hd, :, 0:F], kv[hd, :, F : F + D])
        out[r] = acc


def sums_a(pos, kv0, kv2):
    return call(sums_a_kernel, shape(NX, SR, F), vmem(2), vmem(1)[0], (pos, kv0, kv2))


def sums_b_kernel(pos, kv1, kv3, part, *outs):
    for r in range(NX):
        hd = mod4(pos[0] + r)
        acc = part[r]
        for kv in (kv1, kv3):
            acc = acc + block_state(kv[hd, :, 0:F], kv[hd, :, F : F + D])
        outs[r][...] = acc


def sums_b(pos, kv1, kv3, part):
    return call(sums_b_kernel, [shape(SR, F)] * NX, vmem(3), vmem(NX), (pos, kv1, kv3, part))


def full_state(ref):
    return jnp.concatenate([ref[0:D, :], jnp.broadcast_to(ref[D : D + 1, :], (D, F))], axis=0)


def augmented(v):
    return jnp.concatenate([v, jnp.ones((TB, D), BF)], axis=1)


def causal_mask():
    t = lax.broadcasted_iota(jnp.int32, (TB, TB), 0)
    s = lax.broadcasted_iota(jnp.int32, (TB, TB), 1)
    return s <= t


def order_sums(z, parts, reverse):
    out = []
    for b in range(NZ):
        acc = jnp.zeros(parts[0].shape, F32)
        for o in range(NZ):
            if o == b:
                continue
            mine, other = mod4(z - b), mod4(z - o)
            take = (other > mine) if reverse else (other < mine)
            acc = acc + parts[o] * take.astype(F32)
        out.append(acc)
    return out


def rows_of(x):
    return jnp.concatenate(split(x), axis=0)


def halves(x):
    n = x.shape[0] // 2
    return x[:n] + x[n:]


def lines_kernel(pos, *refs):
    kvs, l_out = refs[0:4], refs[4]
    x, z = pos[0], pos[1]
    for r in range(HL):
        hd = mod4(x - r)
        parts = [block_state(kvs[b][hd, :, 0:F], kvs[b][hd, :, F : F + D]) for b in range(NZ)]
        for b, line in enumerate(order_sums(z, parts, False)):
            l_out[r, b] = line


def earlier_in_line(pos, kvs):
    return call(lines_kernel, shape(HL, NZ, SR, F), vmem(4), vmem(1)[0], (pos, *kvs))


def pre_kernel(pos, *refs):
    kvs, qs, lines, nd_out = refs[0:4], refs[4:8], refs[8], refs[9]
    x = pos[0]
    mask = causal_mask()
    for r in range(HL):
        hd = mod4(x - r)
        for b in range(NZ):
            q, k = qs[b][hd], kvs[b][hd, :, 0:F]
            va = augmented(kvs[b][hd, :, F : F + D])
            st_hi, st_lo = split(full_state(lines[r, b]))
            sc = rows_of(jnp.where(mask, nt(q, k), 0.0))
            nd_out[r, b] = halves(nn(sc, va)) + nt(q, st_hi) + nt(q, st_lo)


def pre(pos, kvs, qs, lines):
    return call(pre_kernel, shape(HL, NZ, TB, 2 * D), vmem(9), vmem(1)[0], (pos, *kvs, *qs, lines))


PR = 32


def post_kernel(pos, *refs):
    qs, nd, teas, states = refs[0:4], refs[4], refs[5:9], refs[9:13]
    dhi_out, dlo_out, adj_out, sums, both_s = refs[13], refs[14], refs[15], refs[16:20], refs[20]
    x, z = pos[0], pos[1]
    for r in range(HL):
        hd = mod4(x - r)
        e_hi, e_lo = split(full_state(states[r]))
        total = jnp.zeros((SR, F), F32)
        for b in range(NZ):
            q = qs[b][hd]
            held = both_s.at[b % 2]
            held[...] = nd[r, b] + nt(q, e_hi) + nt(q, e_lo)
            for i in range(TB // PR):
                rows = slice(i * PR, (i + 1) * PR)
                inverse = 1.0 / held[rows, D:]
                student = held[rows, 0:D] * inverse
                there = pl.ds(pl.multiple_of(mod4(z - b) * TB + i * PR, PR), PR)
                resid = student - teas[r][there, :].astype(F32)
                n_hi, n_lo = split(resid * inverse)
                dd = -jnp.sum(resid * student, axis=1, keepdims=True) * inverse
                c_hi, c_lo = split(dd * (1.0 / D))
                dhi_out[r, b, rows, 0:D] = n_hi
                dhi_out[r, b, rows, D:] = c_hi
                dlo_out[r, b, rows, 0:D] = n_lo
                dlo_out[r, b, rows, D:] = c_lo
            sides = tn(jnp.concatenate([dhi_out[r, b, :, 0:D], dlo_out[r, b, :, 0:D]], axis=1), q)
            ends = tn(dhi_out[r, b, :, D : D + 8], q) + tn(dlo_out[r, b, :, D : D + 8], q)
            adj = jnp.concatenate([sides[0:D] + sides[D:], ends], axis=0)
            adj_out[r, b] = adj
            total = total + adj
        sums[(-r) % NX][...] = total


def post(pos, qs, nd, teas, states):
    out = call(
        post_kernel,
        [shape(HL, NZ, TB, 2 * D, kind=BF)] * 2 + [shape(HL, NZ, SR, F)] + [shape(SR, F)] * NX,
        vmem(13),
        vmem(3 + NX),
        (pos, *qs, nd, *teas, *states),
        [pltpu.VMEM((2, TB, 2 * D), F32)],
    )
    return out[0], out[1], out[2], out[3:7]


def qgrad_kernel(scale, blocks, pos, *refs):
    n = len(blocks)
    kvs, dhi, dlo, lines, states = refs[0:n], refs[n], refs[n + 1], refs[n + 2], refs[n + 3 : n + 7]
    outs, mixed_out = refs[n + 7 : 2 * n + 7], refs[2 * n + 7]
    x = pos[0]
    mask = causal_mask()
    for r in range(HL):
        hd = mod4(x - r)
        for i, b in enumerate(blocks):
            k = kvs[i][hd, :, 0:F]
            va = augmented(kvs[i][hd, :, F : F + D])
            d_hi = dhi[r, b]
            d_rows = jnp.concatenate([d_hi, dlo[r, b]], axis=0)
            mixed = rows_of(jnp.where(mask, halves(nt(d_rows, va)), 0.0))
            mixed_out[r, i] = mixed
            st_hi, st_lo = split(full_state(states[r][...] + lines[r, b]))
            qg = halves(nn(mixed, k) + nn(d_rows, st_hi)) + nn(d_hi, st_lo)
            outs[i][hd] = (qg * scale).astype(BF)


def qgrad(pos, kvs, dhi, dlo, lines, states, scale, blocks):
    n = len(blocks)
    out = call(
        functools.partial(qgrad_kernel, scale, blocks),
        [piece(F)] * n + [shape(HL, n, 2 * TB, TB, kind=BF)],
        vmem(n + 7),
        vmem(n + 1),
        (pos, *[kvs[b] for b in blocks], dhi, dlo, lines, *states),
    )
    return out[0:n], out[n]


NEAR = (1, 3)


def inner_kernel(pos, *refs):
    kvs, qs, far, near, own, adj, out = refs[0:4], refs[4:8], refs[8], refs[9], refs[10], refs[11], refs[12]
    held = {2: (far, 0), 0: (own, 0), 1: (near, 0), 3: (near, 1)}
    x, z = pos[0], pos[1]
    for r in range(HL):
        hd = mod4(x - r)
        lines = order_sums(z, [adj[r, b] for b in range(NZ)], True)
        for b in range(NZ):
            q = qs[b][hd]
            va = augmented(kvs[b][hd, :, F : F + D])
            mixed = held[b][0].at[r, held[b][1]]
            a_hi, a_lo = split(full_state(lines[b]))
            out[r, b] = tn(mixed[0:TB, :], q) + tn(mixed[TB:, :], q) + nn(va, a_hi) + nn(va, a_lo)


def inner(pos, kvs, qs, far, near, own, adj):
    return call(inner_kernel, shape(HL, NZ, TB, F), vmem(12), vmem(1)[0], (pos, *kvs, *qs, far, near, own, adj))


def last_kernel(scale, blocks, pos, *refs):
    n = len(blocks)
    kvs, part, states, outs = refs[0:n], refs[n], refs[n + 1 : n + 5], refs[n + 5 :]
    x = pos[0]
    for r in range(HL):
        hd = mod4(x - r)
        a_hi, a_lo = split(full_state(states[r]))
        for i, b in enumerate(blocks):
            va = augmented(kvs[i][hd, :, F : F + D])
            kg = part[r, b] + nn(va, a_hi) + nn(va, a_lo)
            outs[i][hd] = (kg * scale).astype(BF)


def last(pos, kvs, part, states, scale, blocks):
    n = len(blocks)
    return call(
        functools.partial(last_kernel, scale, blocks),
        [piece(F)] * n,
        vmem(n + 5),
        vmem(n),
        (pos, *[kvs[b] for b in blocks], part, *states),
    )


def send_z(part, r):
    return lax.ppermute(part, "grp", grp_pairs(0, r))


def send_x(part, r):
    return lax.ppermute(part, "grp", grp_pairs(r, 0))


def exchange_z(parts):
    far, up, down = send_z(parts[2], 2), send_z(parts[1], 1), send_z(parts[3], 3)
    return [parts[0], up, far, down]


def exchange_x(parts):
    far, up, down = send_x(parts[2], 2), send_x(parts[1], 1), send_x(parts[3], 3)
    return [parts[0], up, far, down]


def total_kernel(m0, m1, m2, m3, out):
    out[...] = (m0[...] + m1[...]) + (m2[...] + m3[...])


def chip_kernel(pos, total, other, out, half):
    out[...] = total[...] + other[...]
    half[...] = out[pl.ds(pl.multiple_of(pos[3] * (SR - YR), 8), YR), :]


def spans_kernel(reverse, pos, near, far, out):
    y, c = pos[2], pos[3]

    def wanted(at):
        return ((at > y) if reverse else (at < y)).astype(F32)

    out[...] = near[...] * wanted(mod4(y - 1 + 2 * c))
    far_wanted = wanted(mod4(y + 2))
    mine = c.astype(F32)
    out[0:YR, :] += far[...] * (far_wanted * (1.0 - mine))
    out[YR:SR, :] += far[2 * YR - SR :, :] * (far_wanted * mine)


def back_kernel(reverse, pos, base_a, base_b, other, *refs):
    mine, outs = refs[0:NX], refs[NX:]
    x, c = pos[0], pos[3]
    second = (c == (0 if reverse else 1)).astype(F32)
    base = base_a[...] + base_b[...] + other[...] * second
    for r in range(NX):
        to = mod4(x + r)
        acc = base
        for s in range(NX):
            at = mod4(x - s)
            take = (at > to) if reverse else (at < to)
            acc = acc + mine[s][...] * take.astype(F32)
        outs[r][...] = acc


def scan_states(sums, pos, reverse):
    one = shape(SR, F)
    mine = exchange_x(sums)
    total = call(total_kernel, one, vmem(4), vmem(1)[0], mine)
    other = lax.ppermute(total, "ctx", CORE_PAIRS)
    chip, half = call(chip_kernel, [one, shape(YR, F)], vmem(2), vmem(2), (pos, total, other))
    far = lax.ppermute(half, "ctx", y_pairs(2))
    near = lax.ppermute(chip, "ctx", y_pairs(1))
    base = call(functools.partial(spans_kernel, reverse), one, vmem(2), vmem(1)[0], (pos, near, far))
    base_other = lax.ppermute(base, "ctx", CORE_PAIRS)
    back = call(
        functools.partial(back_kernel, reverse),
        [one] * NX,
        vmem(3 + NX),
        vmem(NX),
        (pos, base, base_other, other, *mine),
    )
    return exchange_x(back)


def local_step(query_feat, key_feat, values, teacher):
    total_tokens = query_feat.shape[0] * lax.axis_size("ctx") * lax.axis_size("grp")
    scale = float(total_tokens) ** 0.5
    pos = HERE
    query_feat, key_feat, values, teacher = (
        pltpu.with_memory_space_constraint(a, pltpu.HBM) for a in (query_feat, key_feat, values, teacher)
    )
    kv = [None] * NZ
    (kv[2],) = pack_kv(key_feat, values, (2,))
    kv[1], kv[3] = pack_kv(key_feat, values, (1, 3))
    (kv[0],) = pack_kv(key_feat, values, (0,))
    kvs = exchange_z(kv)
    q = [None] * NZ
    q[2], q[1], q[3] = pack_q(pos, query_feat, (2, 1, 3))
    (q[0],) = pack_q(pos, query_feat, (0,))
    qs = exchange_z(q)
    teas = exchange_x(pack_teacher(pos, teacher))
    sums = sums_b(pos, kvs[1], kvs[3], sums_a(pos, kvs[0], kvs[2]))
    lines = earlier_in_line(pos, kvs)
    nd = pre(pos, kvs, qs, lines)
    states = scan_states(sums, pos, False)
    d_hi, d_lo, adj, adj_sums = post(pos, qs, nd, teas, states)
    qparts = [None] * NZ
    (qparts[2],), far = qgrad(pos, kvs, d_hi, d_lo, lines, states, scale, (2,))
    (qparts[3], qparts[1]), near = qgrad(pos, kvs, d_hi, d_lo, lines, states, scale, NEAR)
    (qparts[0],), own = qgrad(pos, kvs, d_hi, d_lo, lines, states, scale, (0,))
    query_grad = unpack_all(pos, exchange_z(qparts))
    part = inner(pos, kvs, qs, far, near, own, adj)
    after = scan_states(adj_sums, pos, True)
    kg = [None] * NZ
    (kg[2],) = last(pos, kvs, part, after, scale, (2,))
    kg[3], kg[1] = last(pos, kvs, part, after, scale, (1, 3))
    (kg[0],) = last(pos, kvs, part, after, scale, (0,))
    key_grad = unpack_all(pos, exchange_z(kg))
    return query_grad, key_grad


def solution(mesh):
    placed = (
        P(("ctx", "grp"), None),
        P(("ctx", "grp"), None),
        P(("ctx", "grp"), None),
        P("ctx", "grp"),
    )
    return jax.shard_map(
        local_step,
        mesh=mesh,
        in_specs=placed,
        out_specs=(P(("ctx", "grp"), None), P(("ctx", "grp"), None)),
        check_vma=False,
    )
```

```python
import functools

import jax
import jax.numpy as jnp
from jax import lax
from jax.experimental import pallas as pl
from jax.experimental.pallas import tpu as pltpu
from jax.sharding import PartitionSpec as P


NX, NZ, NY = 4, 4, 4
HL = 4
YR = 72
TB = 256
F = 256
D = 128
SR = D + 8
BF, F32 = jnp.bfloat16, jnp.float32
VMEM_LIMIT = 12 * 1024 * 1024


def grp_pairs(dx, dz):
    return [(x * NZ + z, ((x + dx) % NX) * NZ + (z + dz) % NZ) for x in range(NX) for z in range(NZ)]


def y_pairs(d):
    return [(y * 2 + c, ((y + (d if c == 0 else -d)) % NY) * 2 + c) for y in range(NY) for c in range(2)]


CORE_PAIRS = [(y * 2 + c, y * 2 + 1 - c) for y in range(NY) for c in range(2)]


def params():
    return pltpu.CompilerParams(vmem_limit_bytes=VMEM_LIMIT)


def nn(a, b):
    return lax.dot_general(a, b, (((1,), (0,)), ((), ())), preferred_element_type=F32)


def nt(a, b):
    return lax.dot_general(a, b, (((1,), (1,)), ((), ())), preferred_element_type=F32)


def tn(a, b):
    return lax.dot_general(a, b, (((0,), (0,)), ((), ())), preferred_element_type=F32)


def split(x):
    hi = x.astype(BF)
    rest = x - hi.astype(F32)
    mid = rest.astype(BF)
    return hi, mid, (rest - mid.astype(F32)).astype(BF)


def mod4(a):
    return lax.rem(a + 8, 4)


def vmem(n):
    return [pl.BlockSpec(memory_space=pltpu.VMEM)] * n


def hbm(n):
    return [pl.BlockSpec(memory_space=pltpu.HBM)] * n


HERE = object()


def here():
    g, t = lax.axis_index("grp").astype(jnp.int32), lax.axis_index("ctx").astype(jnp.int32)
    return lax.div(g, NZ), lax.rem(g, NZ), lax.div(t, 2), lax.rem(t, 2)


def shape(*dims, kind=F32):
    return jax.ShapeDtypeStruct(dims, kind)


def piece(cols):
    return shape(HL, TB, cols, kind=BF)


def call(kernel, out_shape, in_specs, out_specs, args, scratch=()):
    body = kernel
    if args[0] is HERE:
        args = args[1:]

        def body(*refs):
            kernel(here(), *refs)

    return pl.pallas_call(
        body,
        out_shape=out_shape,
        in_specs=in_specs,
        out_specs=out_specs,
        scratch_shapes=list(scratch),
        compiler_params=params(),
    )(*args)


def run_copies(copies):
    for c in copies:
        c.start()
    for c in copies:
        c.wait()


def pack_kv_kernel(shifts, k_ref, v_ref, *refs):
    outs, sem = refs[:-1], refs[-1]
    z = lax.rem(lax.axis_index("grp").astype(jnp.int32), NZ)
    copies = []
    for i, r in enumerate(shifts):
        zd = mod4(z + r)
        for j in range(HL):
            kc = pl.ds(pl.multiple_of((j * NZ + zd) * F, F), F)
            vc = pl.ds(pl.multiple_of((j * NZ + zd) * D, D), D)
            copies.append(pltpu.make_async_copy(k_ref.at[:, kc], outs[i].at[j, :, 0:F], sem.at[i, j, 0]))
            copies.append(pltpu.make_async_copy(v_ref.at[:, vc], outs[i].at[j, :, F : F + D], sem.at[i, j, 1]))
    run_copies(copies)


def pack_kv(k, v, shifts):
    n = len(shifts)
    return call(
        functools.partial(pack_kv_kernel, shifts),
        [piece(F + D)] * n,
        hbm(2),
        vmem(n),
        (k, v),
        [pltpu.SemaphoreType.DMA((n, HL, 2))],
    )


def pack_q_kernel(shifts, pos, q_ref, *refs):
    outs, sem = refs[:-1], refs[-1]
    z = pos[1]
    copies = []
    for i, r in enumerate(shifts):
        for j in range(HL):
            qc = pl.ds(pl.multiple_of((j * NZ + mod4(z + r)) * F, F), F)
            copies.append(pltpu.make_async_copy(q_ref.at[:, qc], outs[i].at[j], sem.at[i, j]))
    run_copies(copies)


def pack_q(pos, q, shifts):
    n = len(shifts)
    return call(
        functools.partial(pack_q_kernel, shifts),
        [piece(F)] * n,
        hbm(1),
        vmem(n),
        (pos, q),
        [pltpu.SemaphoreType.DMA((n, HL))],
    )


def pack_teacher_kernel(pos, t_ref, *refs):
    outs, sem = refs[:-1], refs[-1]
    n = NZ * TB
    copies = []
    for r in range(NX):
        rows = pl.ds(pl.multiple_of(mod4(pos[0] + r) * n, n), n)
        copies.append(pltpu.make_async_copy(t_ref.at[rows, :], outs[r], sem.at[r]))
    run_copies(copies)


def pack_teacher(pos, teacher):
    return call(
        pack_teacher_kernel,
        [shape(NZ * TB, D, kind=BF)] * NX,
        hbm(1),
        vmem(NX),
        (pos, teacher),
        [pltpu.SemaphoreType.DMA((NX,))],
    )


UR = 64


def unpack_kernel(pos, *refs):
    parts, out, held, sem = refs[0:NZ], refs[NZ], refs[NZ + 1], refs[NZ + 2]
    z = pos[1]
    copies = []
    for i in range(TB // UR):
        rows = slice(i * UR, (i + 1) * UR)
        for r in range(NZ):
            for j in range(HL):
                held[rows, pl.ds(pl.multiple_of((j * NZ + mod4(z - r)) * F, F), F)] = parts[r][j, rows, :]
        copies.append(pltpu.make_async_copy(held.at[rows, :], out.at[rows, :], sem.at[i]))
        copies[-1].start()
    for c in copies:
        c.wait()


def unpack_all(pos, parts):
    return call(
        unpack_kernel,
        shape(TB, HL * NZ * F, kind=BF),
        vmem(NZ),
        hbm(1)[0],
        (pos, *parts),
        [pltpu.VMEM((TB, HL * NZ * F), BF), pltpu.SemaphoreType.DMA((TB // UR,))],
    )


def block_state(k, v):
    return jnp.concatenate([tn(v, k), nn(jnp.ones((8, TB), BF), k)], axis=0)


def sums_a_kernel(pos, kv0, kv2, out):
    for r in range(NX):
        hd = mod4(pos[0] + r)
        acc = jnp.zeros((SR, F), F32)
        for kv in (kv0, kv2):
            acc = acc + block_state(kv[hd, :, 0:F], kv[hd, :, F : F + D])
        out[r] = acc


def sums_a(pos, kv0, kv2):
    return call(sums_a_kernel, shape(NX, SR, F), vmem(2), vmem(1)[0], (pos, kv0, kv2))


def sums_b_kernel(pos, kv1, kv3, part, *outs):
    for r in range(NX):
        hd = mod4(pos[0] + r)
        acc = part[r]
        for kv in (kv1, kv3):
            acc = acc + block_state(kv[hd, :, 0:F], kv[hd, :, F : F + D])
        outs[r][...] = acc


def sums_b(pos, kv1, kv3, part):
    return call(sums_b_kernel, [shape(SR, F)] * NX, vmem(3), vmem(NX), (pos, kv1, kv3, part))


def full_state(ref):
    return jnp.concatenate([ref[0:D, :], jnp.broadcast_to(ref[D : D + 1, :], (D, F))], axis=0)


def augmented(v):
    return jnp.concatenate([v, jnp.ones((TB, D), BF)], axis=1)


def causal_mask():
    t = lax.broadcasted_iota(jnp.int32, (TB, TB), 0)
    s = lax.broadcasted_iota(jnp.int32, (TB, TB), 1)
    return s <= t


def order_sums(z, parts, reverse):
    out = []
    for b in range(NZ):
        acc = jnp.zeros(parts[0].shape, F32)
        for o in range(NZ):
            if o == b:
                continue
            mine, other = mod4(z - b), mod4(z - o)
            take = (other > mine) if reverse else (other < mine)
            acc = acc + parts[o] * take.astype(F32)
        out.append(acc)
    return out


def rows_of(x):
    return jnp.concatenate(split(x), axis=0)


def thirds(x):
    n = x.shape[0] // 3
    return x[:n] + (x[n : 2 * n] + x[2 * n :])


def lines_kernel(pos, *refs):
    kvs, l_out = refs[0:4], refs[4]
    x, z = pos[0], pos[1]
    for r in range(HL):
        hd = mod4(x - r)
        parts = [block_state(kvs[b][hd, :, 0:F], kvs[b][hd, :, F : F + D]) for b in range(NZ)]
        for b, line in enumerate(order_sums(z, parts, False)):
            l_out[r, b] = line


def earlier_in_line(pos, kvs):
    return call(lines_kernel, shape(HL, NZ, SR, F), vmem(4), vmem(1)[0], (pos, *kvs))


def pre_kernel(pos, *refs):
    kvs, qs, lines, nd_out = refs[0:4], refs[4:8], refs[8], refs[9]
    x = pos[0]
    mask = causal_mask()
    for r in range(HL):
        hd = mod4(x - r)
        for b in range(NZ):
            q, k = qs[b][hd], kvs[b][hd, :, 0:F]
            va = augmented(kvs[b][hd, :, F : F + D])
            st_hi, st_mid, st_lo = split(full_state(lines[r, b]))
            sc = rows_of(jnp.where(mask, nt(q, k), 0.0))
            nd_out[r, b] = thirds(nn(sc, va)) + (nt(q, st_hi) + (nt(q, st_mid) + nt(q, st_lo)))


def pre(pos, kvs, qs, lines):
    return call(pre_kernel, shape(HL, NZ, TB, 2 * D), vmem(9), vmem(1)[0], (pos, *kvs, *qs, lines))


PR = 32


def post_kernel(pos, *refs):
    qs, nd, teas, states = refs[0:4], refs[4], refs[5:9], refs[9:13]
    d_out, adj_out, sums, both_s = refs[13], refs[14], refs[15:19], refs[19]
    x, z = pos[0], pos[1]
    for r in range(HL):
        hd = mod4(x - r)
        e_hi, e_mid, e_lo = split(full_state(states[r]))
        total = jnp.zeros((SR, F), F32)
        for b in range(NZ):
            q = qs[b][hd]
            held = both_s.at[b % 2]
            held[...] = nd[r, b] + (nt(q, e_hi) + (nt(q, e_mid) + nt(q, e_lo)))
            for i in range(TB // PR):
                rows = slice(i * PR, (i + 1) * PR)
                inverse = 1.0 / held[rows, D:]
                student = held[rows, 0:D] * inverse
                there = pl.ds(pl.multiple_of(mod4(z - b) * TB + i * PR, PR), PR)
                resid = student - teas[r][there, :].astype(F32)
                dd = -jnp.sum(resid * student, axis=1, keepdims=True) * inverse
                for t, (n, c) in enumerate(zip(split(resid * inverse), split(dd * (1.0 / D)))):
                    out_rows = slice(t * TB + i * PR, t * TB + (i + 1) * PR)
                    d_out[r, b, out_rows, 0:D] = n
                    d_out[r, b, out_rows, D:] = c
            terms = [d_out[r, b, t * TB : (t + 1) * TB, :] for t in range(3)]
            sides = thirds(tn(jnp.concatenate([d[:, 0:D] for d in terms], axis=1), q))
            ends = [tn(d[:, D : D + 8], q) for d in terms]
            adj = jnp.concatenate([sides, ends[0] + (ends[1] + ends[2])], axis=0)
            adj_out[r, b] = adj
            total = total + adj
        sums[(-r) % NX][...] = total


def post(pos, qs, nd, teas, states):
    out = call(
        post_kernel,
        [shape(HL, NZ, 3 * TB, 2 * D, kind=BF), shape(HL, NZ, SR, F)] + [shape(SR, F)] * NX,
        vmem(13),
        vmem(2 + NX),
        (pos, *qs, nd, *teas, *states),
        [pltpu.VMEM((2, TB, 2 * D), F32)],
    )
    return out[0], out[1], out[2:6]


def qgrad_kernel(scale, blocks, pos, *refs):
    n = len(blocks)
    kvs, d, lines, states = refs[0:n], refs[n], refs[n + 1], refs[n + 2 : n + 6]
    outs, mixed_out = refs[n + 6 : 2 * n + 6], refs[2 * n + 6]
    x = pos[0]
    mask = causal_mask()
    for r in range(HL):
        hd = mod4(x - r)
        for i, b in enumerate(blocks):
            k = kvs[i][hd, :, 0:F]
            va = augmented(kvs[i][hd, :, F : F + D])
            d_rows = d[r, b]
            mixed = rows_of(jnp.where(mask, thirds(nt(d_rows, va)), 0.0))
            mixed_out[r, i] = mixed
            st_hi, st_mid, st_lo = split(full_state(states[r][...] + lines[r, b]))
            small = nn(d_rows[0 : 2 * TB], st_mid)
            small = small[0:TB] + (small[TB:] + nn(d_rows[0:TB], st_lo))
            qg = thirds(nn(mixed, k) + nn(d_rows, st_hi)) + small
            outs[i][hd] = (qg * scale).astype(BF)


def qgrad(pos, kvs, d, lines, states, scale, blocks):
    n = len(blocks)
    out = call(
        functools.partial(qgrad_kernel, scale, blocks),
        [piece(F)] * n + [shape(HL, n, 3 * TB, TB, kind=BF)],
        vmem(n + 6),
        vmem(n + 1),
        (pos, *[kvs[b] for b in blocks], d, lines, *states),
    )
    return out[0:n], out[n]


NEAR = (1, 3)


def inner_kernel(pos, *refs):
    kvs, qs, far, near, own, adj, out = refs[0:4], refs[4:8], refs[8], refs[9], refs[10], refs[11], refs[12]
    held = {2: (far, 0), 0: (own, 0), 1: (near, 0), 3: (near, 1)}
    x, z = pos[0], pos[1]
    for r in range(HL):
        hd = mod4(x - r)
        lines = order_sums(z, [adj[r, b] for b in range(NZ)], True)
        for b in range(NZ):
            q = qs[b][hd]
            va = augmented(kvs[b][hd, :, F : F + D])
            mixed = held[b][0].at[r, held[b][1]]
            kg = [tn(mixed[t * TB : (t + 1) * TB, :], q) for t in range(3)]
            kg += [nn(va, a) for a in split(full_state(lines[b]))]
            out[r, b] = (kg[0] + kg[3]) + ((kg[1] + kg[4]) + (kg[2] + kg[5]))


def inner(pos, kvs, qs, far, near, own, adj):
    return call(inner_kernel, shape(HL, NZ, TB, F), vmem(12), vmem(1)[0], (pos, *kvs, *qs, far, near, own, adj))


def last_kernel(scale, blocks, pos, *refs):
    n = len(blocks)
    kvs, part, states, outs = refs[0:n], refs[n], refs[n + 1 : n + 5], refs[n + 5 :]
    x = pos[0]
    for r in range(HL):
        hd = mod4(x - r)
        a_hi, a_mid, a_lo = split(full_state(states[r]))
        for i, b in enumerate(blocks):
            va = augmented(kvs[i][hd, :, F : F + D])
            kg = part[r, b] + (nn(va, a_hi) + (nn(va, a_mid) + nn(va, a_lo)))
            outs[i][hd] = (kg * scale).astype(BF)


def last(pos, kvs, part, states, scale, blocks):
    n = len(blocks)
    return call(
        functools.partial(last_kernel, scale, blocks),
        [piece(F)] * n,
        vmem(n + 5),
        vmem(n),
        (pos, *[kvs[b] for b in blocks], part, *states),
    )


def send_z(part, r):
    return lax.ppermute(part, "grp", grp_pairs(0, r))


def send_x(part, r):
    return lax.ppermute(part, "grp", grp_pairs(r, 0))


def exchange_z(parts):
    far, up, down = send_z(parts[2], 2), send_z(parts[1], 1), send_z(parts[3], 3)
    return [parts[0], up, far, down]


def exchange_x(parts):
    far, up, down = send_x(parts[2], 2), send_x(parts[1], 1), send_x(parts[3], 3)
    return [parts[0], up, far, down]


def total_kernel(m0, m1, m2, m3, out):
    out[...] = (m0[...] + m1[...]) + (m2[...] + m3[...])


def chip_kernel(pos, total, other, out, half):
    out[...] = total[...] + other[...]
    half[...] = out[pl.ds(pl.multiple_of(pos[3] * (SR - YR), 8), YR), :]


def spans_kernel(reverse, pos, near, far, out):
    y, c = pos[2], pos[3]

    def wanted(at):
        return ((at > y) if reverse else (at < y)).astype(F32)

    out[...] = near[...] * wanted(mod4(y - 1 + 2 * c))
    far_wanted = wanted(mod4(y + 2))
    mine = c.astype(F32)
    out[0:YR, :] += far[...] * (far_wanted * (1.0 - mine))
    out[YR:SR, :] += far[2 * YR - SR :, :] * (far_wanted * mine)


def back_kernel(reverse, pos, base_a, base_b, other, *refs):
    mine, outs = refs[0:NX], refs[NX:]
    x, c = pos[0], pos[3]
    second = (c == (0 if reverse else 1)).astype(F32)
    base = base_a[...] + base_b[...] + other[...] * second
    for r in range(NX):
        to = mod4(x + r)
        acc = base
        for s in range(NX):
            at = mod4(x - s)
            take = (at > to) if reverse else (at < to)
            acc = acc + mine[s][...] * take.astype(F32)
        outs[r][...] = acc


def scan_states(sums, pos, reverse):
    one = shape(SR, F)
    mine = exchange_x(sums)
    total = call(total_kernel, one, vmem(4), vmem(1)[0], mine)
    other = lax.ppermute(total, "ctx", CORE_PAIRS)
    chip, half = call(chip_kernel, [one, shape(YR, F)], vmem(2), vmem(2), (pos, total, other))
    far = lax.ppermute(half, "ctx", y_pairs(2))
    near = lax.ppermute(chip, "ctx", y_pairs(1))
    base = call(functools.partial(spans_kernel, reverse), one, vmem(2), vmem(1)[0], (pos, near, far))
    base_other = lax.ppermute(base, "ctx", CORE_PAIRS)
    back = call(
        functools.partial(back_kernel, reverse),
        [one] * NX,
        vmem(3 + NX),
        vmem(NX),
        (pos, base, base_other, other, *mine),
    )
    return exchange_x(back)


def local_step(query_feat, key_feat, values, teacher):
    total_tokens = query_feat.shape[0] * lax.axis_size("ctx") * lax.axis_size("grp")
    scale = float(total_tokens) ** 0.5
    pos = HERE
    query_feat, key_feat, values, teacher = (
        pltpu.with_memory_space_constraint(a, pltpu.HBM) for a in (query_feat, key_feat, values, teacher)
    )
    kv = [None] * NZ
    (kv[2],) = pack_kv(key_feat, values, (2,))
    kv[1], kv[3] = pack_kv(key_feat, values, (1, 3))
    (kv[0],) = pack_kv(key_feat, values, (0,))
    kvs = exchange_z(kv)
    q = [None] * NZ
    q[2], q[1], q[3] = pack_q(pos, query_feat, (2, 1, 3))
    (q[0],) = pack_q(pos, query_feat, (0,))
    qs = exchange_z(q)
    teas = exchange_x(pack_teacher(pos, teacher))
    sums = sums_b(pos, kvs[1], kvs[3], sums_a(pos, kvs[0], kvs[2]))
    lines = earlier_in_line(pos, kvs)
    nd = pre(pos, kvs, qs, lines)
    states = scan_states(sums, pos, False)
    d, adj, adj_sums = post(pos, qs, nd, teas, states)
    qparts = [None] * NZ
    (qparts[2],), far = qgrad(pos, kvs, d, lines, states, scale, (2,))
    (qparts[3], qparts[1]), near = qgrad(pos, kvs, d, lines, states, scale, NEAR)
    (qparts[0],), own = qgrad(pos, kvs, d, lines, states, scale, (0,))
    query_grad = unpack_all(pos, exchange_z(qparts))
    part = inner(pos, kvs, qs, far, near, own, adj)
    after = scan_states(adj_sums, pos, True)
    kg = [None] * NZ
    (kg[2],) = last(pos, kvs, part, after, scale, (2,))
    kg[3], kg[1] = last(pos, kvs, part, after, scale, (1, 3))
    (kg[0],) = last(pos, kvs, part, after, scale, (0,))
    key_grad = unpack_all(pos, exchange_z(kg))
    return query_grad, key_grad


def solution(mesh):
    placed = (
        P(("ctx", "grp"), None),
        P(("ctx", "grp"), None),
        P(("ctx", "grp"), None),
        P("ctx", "grp"),
    )
    return jax.shard_map(
        local_step,
        mesh=mesh,
        in_specs=placed,
        out_specs=(P(("ctx", "grp"), None), P(("ctx", "grp"), None)),
        check_vma=False,
    )
```
